256 devices in a mesh: diag: 32 (over y, z_lo, core), tri: 8 (over z_hi, x).
Axes of the slice: x: 4, y: 4, z: 8 (z_hi: 2, z_lo: 4; z = z_hi * 4 + z_lo), core: 2. Of those that a mesh axis runs over, the one named last changes fastest.
Arguments:
- trial_sets: bfloat16 [2, 12, 131072], P(None, None, 'diag'), may hold values from -6 to 6
- tile_values: bfloat16 [32, 8, 192, 128, 128], P('diag', 'tri'), may hold values from -0.0546875 to 0.0546875
- tile_pattern: int32 [32, 8, 2, 192], P('diag', 'tri'), may hold values from 0 to 31, as said below
- tile_count: int32 [32, 8], P('diag', 'tri'), may hold values from 48 to 192, as said below
Outputs:
- images: float32 [2, 12, 131072], P(None, None, ('diag', 'tri'))
The draws below stay inside these ranges and needn't reach their ends.
Inputs may be any that keep to these rules, and one draw needn't show every extreme that they name: `tile_pattern`: within each stored block the live and padding slots name distinct tiles. `tile_count`: some stored block has all 192 slots live.
All inputs are finite; a program needn't handle non-finite values.
Results may differ from the reference program's by a relative error of at most 0.0003.
Values may be sent and summed in bfloat16 or wider, within the bound.
A program may use at most 64 MiB of HBM per device.

```python
import jax
import jax.numpy as jnp
from jax import lax

TILE = 128
SETS = 2
VECS = 12
BLOCK_TILES = 32
OWNER_TILES = 192
ROWS = 131072
N_DIAG = 32
N_TRI = 8


def draw_tile_pattern(key, part):
    owner_keys = jax.random.split(key, N_DIAG * N_TRI)
    chosen = jax.vmap(lambda subkey: jax.random.permutation(subkey, BLOCK_TILES * BLOCK_TILES)[:OWNER_TILES])(owner_keys)
    chosen = chosen.reshape(N_DIAG, N_TRI, OWNER_TILES).astype(jnp.int32)
    return jnp.stack([chosen // BLOCK_TILES, chosen % BLOCK_TILES], axis=2).astype(jnp.int32)


def draw_tile_count(key, part):
    first_key, second_key = jax.random.split(key)
    counts = jax.random.randint(first_key, (N_DIAG * N_TRI,), OWNER_TILES // 4, OWNER_TILES + 1)
    fullest = jax.random.randint(second_key, (), 0, N_DIAG * N_TRI)
    counts = jnp.where(jnp.arange(N_DIAG * N_TRI) == fullest, OWNER_TILES, counts)
    return counts.reshape(N_DIAG, N_TRI).astype(jnp.int32)


def shard_levels(stream_key, extent, cuts, smallest, largest):
    factor_of, own = 1.0, jax.random.fold_in(stream_key, 6)
    for dim, parts in cuts:
        heights = jnp.exp(jax.random.uniform(jax.random.fold_in(own, dim), (parts,), jnp.float32, smallest / len(cuts), largest / len(cuts)))
        factor_of = factor_of * jnp.repeat(heights, extent[dim] // parts).reshape([-1 if axis == dim else 1 for axis in range(len(extent))])
    return factor_of


def centred(key, extent, scale, most, cuts=(), dtype=jnp.bfloat16):
    array = scale * jax.random.normal(key, extent, jnp.float32)
    if cuts:
        array = array * shard_levels(key, extent, cuts, -0.22, 0.18)
    return jnp.clip(array, -most, most).astype(dtype)


def setup_inputs(seed: int = 0) -> dict:
    seeds = jax.random.split(jax.random.key(seed), 5)
    trial_sets = centred(seeds[0], (SETS, VECS, ROWS), 1.0, 6.0, ((2, 32),))
    tile_values = centred(seeds[1], (N_DIAG, N_TRI, OWNER_TILES, TILE, TILE), (2 * N_TRI * OWNER_TILES * TILE // BLOCK_TILES) ** -0.5, 0.0546875, ((0, 32), (1, 8)))
    tile_pattern = draw_tile_pattern(jax.random.fold_in(seeds[4], 71), 0)
    tile_count = draw_tile_count(jax.random.fold_in(seeds[4], 71), 0)
    return {"trial_sets": trial_sets, "tile_values": tile_values, "tile_pattern": tile_pattern, "tile_count": tile_count}


def reference(trial_sets, tile_values, tile_pattern, tile_count):
    set_count, vec_count, row_total = trial_sets.shape
    columns = set_count * vec_count
    grid = trial_sets.astype(jnp.float32).reshape(columns, N_DIAG, BLOCK_TILES, TILE)
    tile_axis = jnp.arange(BLOCK_TILES)
    slot_axis = jnp.arange(OWNER_TILES)

    def per_diag(diag_index):
        row_sum = jnp.zeros((columns, BLOCK_TILES, TILE), jnp.float32)
        col_list = []
        own_block = grid[:, diag_index]
        for tri_index in range(N_TRI):
            tile_data = tile_values[diag_index, tri_index].astype(jnp.float32)
            tile_rows = tile_pattern[diag_index, tri_index, 0]
            tile_cols = tile_pattern[diag_index, tri_index, 1]
            live_mask = (slot_axis < tile_count[diag_index, tri_index]).astype(jnp.float32)
            source = (diag_index - tri_index) % N_DIAG
            held_block = grid[:, source]
            picked_cols = held_block[:, tile_cols, :]
            row_terms = jnp.einsum("nab,vnb->vna", tile_data, picked_cols, precision=lax.Precision.HIGHEST)
            row_hot = (tile_rows[:, None] == tile_axis[None, :]).astype(jnp.float32) * live_mask[:, None]
            row_sum = row_sum + jnp.einsum("vna,nr->vra", row_terms, row_hot, precision=lax.Precision.HIGHEST)
            picked_rows = own_block[:, tile_rows, :]
            col_terms = jnp.einsum("nab,vna->vnb", tile_data, picked_rows, precision=lax.Precision.HIGHEST)
            col_hot = (tile_cols[:, None] == tile_axis[None, :]).astype(jnp.float32) * live_mask[:, None]
            col_list.append(jnp.einsum("vnb,nr->vrb", col_terms, col_hot, precision=lax.Precision.HIGHEST))
        return row_sum, jnp.stack(col_list)

    row_all, col_all = lax.map(per_diag, jnp.arange(N_DIAG))
    combined = row_all
    for tri_index in range(N_TRI):
        combined = combined + jnp.roll(col_all[:, tri_index], -tri_index, axis=0)
    return combined.transpose(1, 0, 2, 3).reshape(set_count, vec_count, row_total)
```

```python
import functools

import jax
import jax.numpy as jnp
from jax import lax
from jax.experimental import pallas as pl
from jax.experimental.pallas import tpu as pltpu
from jax.sharding import PartitionSpec as P

MESH = pl.DeviceIdType.MESH
GROUP = 32


def place(tile):
    return ((tile >> 2) & 3) * 8 + (tile >> 4) * 4 + (tile & 3)


def product_kernel(transposed, pattern, count, x_ref, tiles_ref, out_ref):
    step = pl.program_id(0)

    @pl.when(step == 0)
    def _():
        out_ref[...] = jnp.zeros_like(out_ref)

    live = count[0, 0]
    source, target = (1, 0) if transposed else (0, 1)
    contract = (((1,), (1,)), ((), ())) if transposed else (((1,), (0,)), ((), ()))

    for part in range(GROUP // 8):
        terms = []
        for u in range(8):
            slot = step * GROUP + part * 8 + u
            term = lax.dot_general(
                x_ref[pattern[source, slot]],
                tiles_ref[part * 8 + u],
                contract,
                preferred_element_type=jnp.float32,
            )
            terms.append(jnp.where(slot < live, term, 0.0))
        for u in range(8):
            slot = step * GROUP + part * 8 + u
            where = place(pattern[target, slot])
            out_ref[where] += terms[u]


def product(transposed, pattern, count, x, tiles):
    blocks, columns, size = x.shape
    total = tiles.shape[0]
    return pl.pallas_call(
        functools.partial(product_kernel, transposed),
        out_shape=jax.ShapeDtypeStruct((blocks, columns, size), jnp.float32),
        grid=(total // GROUP,),
        in_specs=[
            pl.BlockSpec(memory_space=pltpu.SMEM),
            pl.BlockSpec(memory_space=pltpu.SMEM),
            pl.BlockSpec((blocks, columns, size), lambda i: (0, 0, 0)),
            pl.BlockSpec((GROUP, size, size), lambda i: (i, 0, 0)),
        ],
        out_specs=pl.BlockSpec((blocks, columns, size), lambda i: (0, 0, 0)),
        cost_estimate=pl.CostEstimate(
            flops=2 * total * columns * size * size,
            bytes_accessed=2 * total * size * size + 6 * blocks * columns * size,
            transcendentals=0,
        ),
        name="row_product" if transposed else "col_product",
    )(pattern, count, x, tiles)


def reduce_kernel(row_ref, col_ref, out_ref, total, got, half, got_half, send, recv, zsem):
    tri = lax.axis_index("tri")
    x, z = tri % 4, tri // 4
    barrier = pltpu.get_barrier_semaphore()
    for d in range(1, 4):
        pl.semaphore_signal(barrier, inc=1, device_id={"tri": z * 4 + (x + d) % 4}, device_id_type=MESH)
    pl.semaphore_signal(barrier, inc=1, device_id={"tri": (1 - z) * 4 + x}, device_id_type=MESH)
    total[...] = row_ref[...] + col_ref[...]
    pl.semaphore_wait(barrier, 4)
    copies = []
    for d in (2, 1, 3):
        peer = (x + d) % 4
        copy = pltpu.make_async_remote_copy(
            src_ref=total.at[pl.ds(peer * 8, 8)],
            dst_ref=got.at[d - 1],
            send_sem=send.at[d - 1],
            recv_sem=recv.at[d - 1],
            device_id={"tri": z * 4 + peer},
            device_id_type=MESH,
        )
        copy.start()
        copies.append(copy)
    for copy in copies:
        copy.wait_recv()
    theirs, mine = (1 - z) * 4, z * 4
    half[0] = total[pl.ds(x * 8 + theirs, 4)] + got[0, pl.ds(theirs, 4)] + got[1, pl.ds(theirs, 4)] + got[2, pl.ds(theirs, 4)]
    half[1] = total[pl.ds(x * 8 + mine, 4)] + got[0, pl.ds(mine, 4)] + got[1, pl.ds(mine, 4)] + got[2, pl.ds(mine, 4)]
    across = pltpu.make_async_remote_copy(
        src_ref=half.at[0],
        dst_ref=got_half,
        send_sem=zsem.at[0],
        recv_sem=zsem.at[1],
        device_id={"tri": (1 - z) * 4 + x},
        device_id_type=MESH,
    )
    across.start()
    for copy in copies:
        copy.wait_send()
    across.wait()
    for j in range(4):
        out_ref[:, j * 128 : (j + 1) * 128] = half[1, j] + got_half[j]


def reduced(row, col):
    blocks, columns, size = row.shape
    return pl.pallas_call(
        reduce_kernel,
        out_shape=jax.ShapeDtypeStruct((columns, blocks * size // 8), jnp.float32),
        in_specs=[pl.BlockSpec(memory_space=pltpu.VMEM)] * 2,
        out_specs=pl.BlockSpec(memory_space=pltpu.VMEM),
        scratch_shapes=[
            pltpu.VMEM((blocks, columns, size), jnp.float32),
            pltpu.VMEM((3, 8, columns, size), jnp.float32),
            pltpu.VMEM((2, 4, columns, size), jnp.float32),
            pltpu.VMEM((4, columns, size), jnp.float32),
            pltpu.SemaphoreType.DMA((3,)),
            pltpu.SemaphoreType.DMA((3,)),
            pltpu.SemaphoreType.DMA((2,)),
        ],
        compiler_params=pltpu.CompilerParams(collective_id=0, has_side_effects=True),
        name="reduce_tri",
    )(row, col)


def local(trial_sets, tile_values, tile_pattern, tile_count):
    sets, vecs, rows = trial_sets.shape
    columns = sets * vecs
    size = tile_values.shape[-1]
    blocks = rows // size
    own = trial_sets.transpose(1, 0, 2).reshape(columns, blocks, size).transpose(1, 0, 2)
    diag, tri = lax.axis_size("diag"), lax.axis_size("tri")
    pairs = [(i * tri + k, (i + k) % diag * tri + k) for i in range(diag) for k in range(tri)]
    held = lax.ppermute(own, ("diag", "tri"), pairs)
    pattern, tiles = tile_pattern[0, 0], tile_values[0, 0]
    col = product(False, pattern, tile_count, own, tiles)
    back = lax.ppermute(col, ("diag", "tri"), [(b, a) for a, b in pairs])
    row = product(True, pattern, tile_count, held, tiles)
    out = reduced(row, back)
    return out.reshape(vecs, sets, rows // tri).transpose(1, 0, 2)


def solution(mesh):
    return jax.shard_map(
        local,
        mesh=mesh,
        in_specs=(
            P(None, None, "diag"),
            P("diag", "tri", None, None, None),
            P("diag", "tri", None, None),
            P("diag", "tri"),
        ),
        out_specs=P(None, None, ("diag", "tri")),
        check_vma=False,
    )
```

```python
import functools

import jax
import jax.numpy as jnp
from jax import lax
from jax.experimental import pallas as pl
from jax.experimental.pallas import tpu as pltpu
from jax.sharding import PartitionSpec as P

MESH = pl.DeviceIdType.MESH
UNROLL = 32
CHUNKS = 8


def depth(i, z_hi):
    return ((i >> 1) & 3) + 4 * z_hi


def near(i, z_hi, s, h):
    gap = (depth(i, z_hi) - depth(s, h)) & 7
    return (gap <= 1) | (gap == 7) | (gap == 2 + 4 * (i & 1))


def tables(pattern, live, place_first):
    rows, cols = pattern[0:1, :], pattern[1:2, :]
    target, source = (rows, cols) if place_first else (cols, rows)
    lane = lax.broadcasted_iota(jnp.int32, (1, 256), 1)
    placed = ((target >> 2) & 3) * 8 + (target >> 4) * 4 + (target & 3)
    word = placed * 8192 + source * 256 + lane
    word = word + jnp.where(lane < live, 0, 1 << 18)
    word = jnp.where(lane < 192, word, (1 << 20) + lane)

    def column(row):
        wide = jnp.broadcast_to(row, (128, 256))
        tall = jnp.concatenate([wide[:, :128].T, wide[:, 128:].T], 0)
        return jnp.concatenate([tall, tall], 1)

    tall = column(word)
    rank = jnp.sum(jnp.where(tall < word, 1, 0), axis=0, keepdims=True)
    spot = column(rank)
    order = jnp.sum(jnp.where(spot == lane, tall, 0), axis=0, keepdims=True)
    below = jnp.sum(jnp.where(tall < (lane + 1) * 8192, 1, 0), axis=0, keepdims=True)
    before = jnp.sum(jnp.where(tall < lane * 8192, 1, 0), axis=0, keepdims=True)
    ends = jnp.where(below == before, 192, below - 1)
    return order, ends


def visit(transposed, row, first, last, acc, table, tiles, xs, runs):
    contract = (((1,), (1,)), ((), ())) if transposed else (((1,), (0,)), ((), ()))
    side = 0 if transposed else 1

    def body(step, acc):
        base = step * UNROLL
        words = [table[row, base + u] for u in range(UNROLL)]
        terms = []
        for u in range(0, UNROLL, 2):
            pair = words[u : u + 2]
            left = jnp.concatenate([xs[(w >> 8) & 31] for w in pair], 0)
            right = jnp.concatenate([tiles[w & 255] for w in pair], side)
            both = lax.dot_general(left, right, contract, preferred_element_type=jnp.float32)
            terms += [both[0:24, 0:128], both[24:48, 128:256]]
        past = table[row, jnp.maximum(base - 1, 0)]
        for u in range(UNROLL):
            same = (words[u] >> 13) == (past >> 13)
            past = words[u]
            acc = terms[u] + jnp.where(same, acc, 0.0)
            runs[base + u] = acc
        return acc

    return lax.fori_loop(first, last, body, acc)


def kernel(
    x_hbm, pattern_hbm, count, tiles_hbm, out_ref,
    raw, pattern, padded, table_v, table, tiles, own, held, runs,
    col, row, col_got, x_got, half, half_got,
    load, tile_sem, x_send, x_recv, col_send, col_recv, row_send, row_recv, z_sem,
):
    i, k = lax.axis_index("diag"), lax.axis_index("tri")
    x, z_hi = k & 3, k >> 2
    source = (i - k) & 31
    home = k == 0
    from_half = jnp.where(near(i, z_hi, source, 0), 0, 1)
    giver = {"diag": source, "tri": from_half * 4 + x}
    takers = []
    for h in (0, 1):
        user = (i + 4 * h + x) & 31
        takes = near(user, h, i, z_hi) & jnp.logical_not((h * 4 + x) == 0)
        takers.append((takes, {"diag": user, "tri": h * 4 + x}))
    peers = [{"diag": i, "tri": z_hi * 4 + ((x + d) & 3)} for d in (1, 2, 3)]
    across = {"diag": i, "tri": k ^ 4}

    barrier = pltpu.get_barrier_semaphore()
    expected = jnp.int32(4)
    for peer in [across, *peers]:
        pl.semaphore_signal(barrier, inc=1, device_id=peer, device_id_type=MESH)
    for takes, user in [*takers, (jnp.logical_not(home), giver)]:
        expected = expected + takes.astype(jnp.int32)

        @pl.when(takes)
        def _():
            pl.semaphore_signal(barrier, inc=1, device_id=user, device_id_type=MESH)

    get_pattern = pltpu.make_async_copy(pattern_hbm, pattern, load.at[0])
    get_x = pltpu.make_async_copy(x_hbm, raw, load.at[1])
    get_pattern.start()
    get_x.start()
    each = 192 // CHUNKS
    get_tiles = []
    for n in range(CHUNKS):
        part = pl.ds(n * each, each)
        get_tiles.append(pltpu.make_async_copy(tiles_hbm.at[part], tiles.at[part], tile_sem.at[n]))
        get_tiles[n].start()

    get_pattern.wait()
    padded[:, 0:192] = pattern[...]
    padded[:, 192:256] = jnp.zeros((2, 64), jnp.int32)
    slots = padded[...]
    live = count[0, 0]
    col_order, col_ends = tables(slots, live, False)
    row_order, row_ends = tables(slots, live, True)
    table_v[...] = jnp.concatenate([col_order, col_ends, row_order, row_ends] * 2, 0)
    runs[192] = jnp.zeros((24, 128), jnp.float32)

    get_x.wait()
    whole = jnp.concatenate([raw[p] for p in range(12)], 0)
    for c in range(32):
        own[c] = whole[:, c * 128 : (c + 1) * 128]
    get_table = pltpu.make_async_copy(table_v, table, load.at[2])
    get_table.start()
    get_table.wait()

    for copy in get_tiles:
        copy.wait()
    acc = jnp.zeros((24, 128), jnp.float32)
    acc = visit(False, 0, 0, 2, acc, table, tiles, own, runs)

    pl.semaphore_wait(barrier, expected)
    give = []
    for h in (0, 1):
        takes, user = takers[h]
        copy = pltpu.make_async_remote_copy(own, held, x_send.at[h], x_recv, device_id=user, device_id_type=MESH)
        give.append(copy)

        @pl.when(takes)
        def _():
            copy.start()

    keep = pltpu.make_async_copy(own, held, x_recv)

    @pl.when(home)
    def _():
        keep.start()

    acc = visit(False, 0, 2, 192 // UNROLL, acc, table, tiles, own, runs)
    for p in range(32):
        col[p] = runs[table[1, p]]

    back = pltpu.make_async_remote_copy(
        col, col_got.at[z_hi], col_send, col_recv.at[z_hi], device_id=giver, device_id_type=MESH
    )

    @pl.when(jnp.logical_not(home))
    def _():
        back.start()
        pltpu.make_async_remote_copy(own, held, x_send.at[0], x_recv, device_id=giver, device_id_type=MESH).wait_recv()

    @pl.when(home)
    def _():
        keep.wait()

    acc = jnp.zeros((24, 128), jnp.float32)
    visit(True, 2, 0, 192 // UNROLL, acc, table, tiles, held, runs)
    for p in range(32):
        row[p] = runs[table[3, p]]

    @pl.when(home)
    def _():
        row[...] += col[...]

    for h in (0, 1):
        takes, user = takers[h]

        @pl.when(takes)
        def _():
            pltpu.make_async_remote_copy(
                col, col_got.at[h], col_send, col_recv.at[h], device_id=user, device_id_type=MESH
            ).wait_recv()
            row[...] += col_got[h]

    scatter = []
    for d in (2, 1, 3):
        to = (x + d) & 3
        copy = pltpu.make_async_remote_copy(
            row.at[pl.ds(to * 8, 8)],
            x_got.at[d - 1],
            row_send.at[d - 1],
            row_recv.at[d - 1],
            device_id={"diag": i, "tri": z_hi * 4 + to},
            device_id_type=MESH,
        )
        copy.start()
        scatter.append(copy)

    for h in (0, 1):
        takes, user = takers[h]

        @pl.when(takes)
        def _():
            give[h].wait_send()

    @pl.when(jnp.logical_not(home))
    def _():
        back.wait_send()

    for copy in scatter:
        copy.wait_recv()
    for n, side in enumerate((1 - z_hi, z_hi)):
        total = row[pl.ds(x * 8 + side * 4, 4)]
        for d in range(3):
            total = total + x_got[d, pl.ds(side * 4, 4)]
        half[n] = total
    swap = pltpu.make_async_remote_copy(
        half.at[0], half_got, z_sem.at[0], z_sem.at[1], device_id=across, device_id_type=MESH
    )
    swap.start()
    for copy in scatter:
        copy.wait_send()
    swap.wait()
    for j in range(4):
        out_ref[:, j * 128 : (j + 1) * 128] = half[1, j] + half_got[j]


def local(trial_sets, tile_values, tile_pattern, tile_count):
    sets, vecs, rows = trial_sets.shape
    tri = lax.axis_size("tri")
    columns = sets * vecs
    slots, size = tile_values.shape[2:4]
    blocks = rows // size
    f32, bf16, i32 = jnp.float32, jnp.bfloat16, jnp.int32
    dma = pltpu.SemaphoreType.DMA
    block = (columns, size)
    out = pl.pallas_call(
        kernel,
        out_shape=jax.ShapeDtypeStruct((columns, rows // tri), f32),
        in_specs=[
            pl.BlockSpec(memory_space=pl.ANY),
            pl.BlockSpec(memory_space=pl.ANY),
            pl.BlockSpec(memory_space=pltpu.SMEM),
            pl.BlockSpec(memory_space=pl.ANY),
        ],
        out_specs=pl.BlockSpec(memory_space=pltpu.VMEM),
        scratch_shapes=[
            pltpu.VMEM((vecs, sets, rows), bf16),
            pltpu.VMEM((2, slots), i32),
            pltpu.VMEM((2, 256), i32),
            pltpu.VMEM((8, 256), i32),
            pltpu.SMEM((8, 256), i32),
            pltpu.VMEM((slots, size, size), bf16),
            pltpu.VMEM((blocks, *block), bf16),
            pltpu.VMEM((blocks, *block), bf16),
            pltpu.VMEM((slots + 8, *block), f32),
            pltpu.VMEM((blocks, *block), f32),
            pltpu.VMEM((blocks, *block), f32),
            pltpu.VMEM((2, blocks, *block), f32),
            pltpu.VMEM((3, 8, *block), f32),
            pltpu.VMEM((2, 4, *block), f32),
            pltpu.VMEM((4, *block), f32),
            dma((3,)),
            dma((CHUNKS,)),
            dma((2,)),
            dma(()),
            dma(()),
            dma((2,)),
            dma((3,)),
            dma((3,)),
            dma((2,)),
        ],
        compiler_params=pltpu.CompilerParams(
            collective_id=0, has_side_effects=True, vmem_limit_bytes=63 << 20
        ),
        name="block_products",
    )(trial_sets.transpose(1, 0, 2), tile_pattern[0, 0], tile_count, tile_values[0, 0])
    return out.reshape(vecs, sets, rows // tri).transpose(1, 0, 2)


def solution(mesh):
    return jax.shard_map(
        local,
        mesh=mesh,
        in_specs=(
            P(None, None, "diag"),
            P("diag", "tri", None, None, None),
            P("diag", "tri", None, None),
            P("diag", "tri"),
        ),
        out_specs=P(None, None, ("diag", "tri")),
        check_vma=False,
    )
```

```python
import functools

import jax
import jax.numpy as jnp
from jax import lax
from jax.experimental import pallas as pl
from jax.experimental.pallas import tpu as pltpu
from jax.sharding import PartitionSpec as P

MESH = pl.DeviceIdType.MESH
UNROLL = 32
CHUNKS = 8


HALVES = (0x2822, 0x8A23, 0x08AB, 0x23AE)


def half_of(i, z_hi, x):
    bits = jnp.where(x < 2, jnp.where(x == 0, HALVES[0], HALVES[1]), jnp.where(x == 2, HALVES[2], HALVES[3]))
    return (bits >> ((i & 7) * 2 + z_hi)) & 1


def tables(pattern, live, place_first):
    rows, cols = pattern[0:1, :], pattern[1:2, :]
    target, source = (rows, cols) if place_first else (cols, rows)
    lane = lax.broadcasted_iota(jnp.int32, (1, 256), 1)
    placed = ((target >> 2) & 3) * 8 + (target >> 4) * 4 + (target & 3)
    word = placed * 8192 + source * 256 + lane
    word = word + jnp.where(lane < live, 0, 1 << 18)
    word = jnp.where(lane < 192, word, (1 << 20) + lane)

    def column(row):
        wide = jnp.broadcast_to(row, (128, 256))
        tall = jnp.concatenate([wide[:, :128].T, wide[:, 128:].T], 0)
        return jnp.concatenate([tall, tall], 1)

    tall = column(word)
    rank = jnp.sum(jnp.where(tall < word, 1, 0), axis=0, keepdims=True)
    spot = column(rank)
    order = jnp.sum(jnp.where(spot == lane, tall, 0), axis=0, keepdims=True)
    below = jnp.sum(jnp.where(tall < (lane + 1) * 8192, 1, 0), axis=0, keepdims=True)
    before = jnp.sum(jnp.where(tall < lane * 8192, 1, 0), axis=0, keepdims=True)
    ends = jnp.where(below == before, 192, below - 1)
    return order, ends


def coded(value):
    scale = jnp.maximum(jnp.max(jnp.abs(value), axis=1, keepdims=True), 4e-34)
    return jnp.round(value * (32767.0 / scale)).astype(jnp.int32).astype(jnp.int16), scale * (1 / 32767.0)


def visit(transposed, row, first, last, acc, table, tiles, xs, runs):
    contract = (((1,), (1,)), ((), ())) if transposed else (((1,), (0,)), ((), ()))
    side = 0 if transposed else 1

    def body(step, acc):
        base = step * UNROLL
        words = [table[row, base + u] for u in range(UNROLL)]
        terms = []
        for u in range(0, UNROLL, 2):
            pair = words[u : u + 2]
            left = jnp.concatenate([xs[(w >> 8) & 31] for w in pair], 0)
            right = jnp.concatenate([tiles[w & 255] for w in pair], side)
            both = lax.dot_general(left, right, contract, preferred_element_type=jnp.float32)
            terms += [both[0:24, 0:128], both[24:48, 128:256]]
        past = table[row, jnp.maximum(base - 1, 0)]
        for u in range(UNROLL):
            same = (words[u] >> 13) == (past >> 13)
            past = words[u]
            acc = terms[u] + jnp.where(same, acc, 0.0)
            runs[base + u] = acc
        return acc

    return lax.fori_loop(first, last, body, acc)


def kernel(
    x_hbm, pattern_hbm, count, tiles_hbm, out_ref,
    raw, pattern, padded, table_v, table, tiles, own, held, runs,
    col, col_scale, row, col_got, scale_got, x_got, half, half_got,
    load, tile_sem, x_send, x_recv, col_send, col_recv, scale_send, scale_recv, row_send, row_recv, z_sem,
):
    i, k = lax.axis_index("diag"), lax.axis_index("tri")
    x, z_hi = k & 3, k >> 2
    source = (i - k) & 31
    home = k == 0
    from_half = half_of(i, z_hi, x)
    giver = {"diag": source, "tri": from_half * 4 + x}
    takers = []
    for h in (0, 1):
        user = (i + 4 * h + x) & 31
        takes = (half_of(user, h, x) == z_hi) & jnp.logical_not((h * 4 + x) == 0)
        takers.append((takes, {"diag": user, "tri": h * 4 + x}))
    peers = [{"diag": i, "tri": z_hi * 4 + ((x + d) & 3)} for d in (1, 2, 3)]
    across = {"diag": i, "tri": k ^ 4}

    barrier = pltpu.get_barrier_semaphore()
    expected = jnp.int32(4)
    for peer in [across, *peers]:
        pl.semaphore_signal(barrier, inc=1, device_id=peer, device_id_type=MESH)
    for takes, user in [*takers, (jnp.logical_not(home), giver)]:
        expected = expected + takes.astype(jnp.int32)

        @pl.when(takes)
        def _():
            pl.semaphore_signal(barrier, inc=1, device_id=user, device_id_type=MESH)

    get_pattern = pltpu.make_async_copy(pattern_hbm, pattern, load.at[0])
    get_x = pltpu.make_async_copy(x_hbm, raw, load.at[1])
    get_pattern.start()
    get_x.start()
    each = 192 // CHUNKS
    get_tiles = []
    for n in range(CHUNKS):
        part = pl.ds(n * each, each)
        get_tiles.append(pltpu.make_async_copy(tiles_hbm.at[part], tiles.at[part], tile_sem.at[n]))
        get_tiles[n].start()

    get_pattern.wait()
    padded[:, 0:192] = pattern[...]
    padded[:, 192:256] = jnp.zeros((2, 64), jnp.int32)
    slots = padded[...]
    live = count[0, 0]
    col_order, col_ends = tables(slots, live, False)
    row_order, row_ends = tables(slots, live, True)
    table_v[...] = jnp.concatenate([col_order, col_ends, row_order, row_ends] * 2, 0)
    runs[192] = jnp.zeros((24, 128), jnp.float32)

    get_x.wait()
    whole = jnp.concatenate([raw[p] for p in range(12)], 0)
    for c in range(32):
        own[c] = whole[:, c * 128 : (c + 1) * 128]
    get_table = pltpu.make_async_copy(table_v, table, load.at[2])
    get_table.start()
    get_table.wait()

    for copy in get_tiles:
        copy.wait()
    acc = jnp.zeros((24, 128), jnp.float32)
    acc = visit(False, 0, 0, 2, acc, table, tiles, own, runs)

    pl.semaphore_wait(barrier, expected)
    give = []
    for h in (0, 1):
        takes, user = takers[h]
        copy = pltpu.make_async_remote_copy(own, held, x_send.at[h], x_recv, device_id=user, device_id_type=MESH)
        give.append(copy)

        @pl.when(takes)
        def _():
            copy.start()

    keep = pltpu.make_async_copy(own, held, x_recv)

    @pl.when(home)
    def _():
        keep.start()

    acc = visit(False, 0, 2, 192 // UNROLL, acc, table, tiles, own, runs)
    lane = lax.broadcasted_iota(jnp.int32, (24, 128), 1)
    scales = jnp.zeros((24, 128), jnp.float32)
    for p in range(32):
        col[p], scale = coded(runs[table[1, p]])
        scales = jnp.where(lane == p, scale, scales)
    col_scale[...] = scales

    back = [
        pltpu.make_async_remote_copy(
            col, col_got.at[z_hi], col_send, col_recv.at[z_hi], device_id=giver, device_id_type=MESH
        ),
        pltpu.make_async_remote_copy(
            col_scale, scale_got.at[z_hi], scale_send, scale_recv.at[z_hi], device_id=giver, device_id_type=MESH
        ),
    ]

    @pl.when(jnp.logical_not(home))
    def _():
        for copy in back:
            copy.start()
        pltpu.make_async_remote_copy(own, held, x_send.at[0], x_recv, device_id=giver, device_id_type=MESH).wait_recv()

    @pl.when(home)
    def _():
        keep.wait()

    acc = jnp.zeros((24, 128), jnp.float32)
    visit(True, 2, 0, 192 // UNROLL, acc, table, tiles, held, runs)
    for p in range(32):
        row[p] = runs[table[3, p]]

    def add(codes, scale):
        scale = scale[...]
        for p in range(32):
            row[p] += codes[p].astype(jnp.int32).astype(jnp.float32) * scale[:, p : p + 1]

    @pl.when(home)
    def _():
        add(col, col_scale)

    for h in (0, 1):
        takes, user = takers[h]

        @pl.when(takes)
        def _():
            pltpu.make_async_remote_copy(
                col, col_got.at[h], col_send, col_recv.at[h], device_id=user, device_id_type=MESH
            ).wait_recv()
            pltpu.make_async_remote_copy(
                col_scale, scale_got.at[h], scale_send, scale_recv.at[h], device_id=user, device_id_type=MESH
            ).wait_recv()
            add(col_got.at[h], scale_got.at[h])

    scatter = []
    for d in (2, 1, 3):
        to = (x + d) & 3
        copy = pltpu.make_async_remote_copy(
            row.at[pl.ds(to * 8, 8)],
            x_got.at[d - 1],
            row_send.at[d - 1],
            row_recv.at[d - 1],
            device_id={"diag": i, "tri": z_hi * 4 + to},
            device_id_type=MESH,
        )
        copy.start()
        scatter.append(copy)

    for h in (0, 1):
        takes, user = takers[h]

        @pl.when(takes)
        def _():
            give[h].wait_send()

    @pl.when(jnp.logical_not(home))
    def _():
        for copy in back:
            copy.wait_send()

    for copy in scatter:
        copy.wait_recv()
    for n, side in enumerate((1 - z_hi, z_hi)):
        total = row[pl.ds(x * 8 + side * 4, 4)]
        for d in range(3):
            total = total + x_got[d, pl.ds(side * 4, 4)]
        half[n] = total
    swap = pltpu.make_async_remote_copy(
        half.at[0], half_got, z_sem.at[0], z_sem.at[1], device_id=across, device_id_type=MESH
    )
    swap.start()
    for copy in scatter:
        copy.wait_send()
    swap.wait()
    for j in range(4):
        total = half[1, j] + half_got[j]
        for p in range(12):
            out_ref[p, :, j * 128 : (j + 1) * 128] = total[2 * p : 2 * p + 2, :]


def local(trial_sets, tile_values, tile_pattern, tile_count):
    sets, vecs, rows = trial_sets.shape
    tri = lax.axis_size("tri")
    columns = sets * vecs
    slots, size = tile_values.shape[2:4]
    blocks = rows // size
    f32, bf16, i32 = jnp.float32, jnp.bfloat16, jnp.int32
    dma = pltpu.SemaphoreType.DMA
    block = (columns, size)
    out = pl.pallas_call(
        kernel,
        out_shape=jax.ShapeDtypeStruct((vecs, sets, rows // tri), f32),
        in_specs=[
            pl.BlockSpec(memory_space=pl.ANY),
            pl.BlockSpec(memory_space=pl.ANY),
            pl.BlockSpec(memory_space=pltpu.SMEM),
            pl.BlockSpec(memory_space=pl.ANY),
        ],
        out_specs=pl.BlockSpec(memory_space=pltpu.VMEM),
        scratch_shapes=[
            pltpu.VMEM((vecs, sets, rows), bf16),
            pltpu.VMEM((2, slots), i32),
            pltpu.VMEM((2, 256), i32),
            pltpu.VMEM((8, 256), i32),
            pltpu.SMEM((8, 256), i32),
            pltpu.VMEM((slots, size, size), bf16),
            pltpu.VMEM((blocks, *block), bf16),
            pltpu.VMEM((blocks, *block), bf16),
            pltpu.VMEM((slots + 8, *block), f32),
            pltpu.VMEM((blocks, *block), jnp.int16),
            pltpu.VMEM(block, f32),
            pltpu.VMEM((blocks, *block), f32),
            pltpu.VMEM((2, blocks, *block), jnp.int16),
            pltpu.VMEM((2, *block), f32),
            pltpu.VMEM((3, 8, *block), f32),
            pltpu.VMEM((2, 4, *block), f32),
            pltpu.VMEM((4, *block), f32),
            dma((3,)),
            dma((CHUNKS,)),
            dma((2,)),
            dma(()),
            dma(()),
            dma((2,)),
            dma(()),
            dma((2,)),
            dma((3,)),
            dma((3,)),
            dma((2,)),
        ],
        compiler_params=pltpu.CompilerParams(
            collective_id=0, has_side_effects=True, vmem_limit_bytes=63 << 20
        ),
        name="block_products",
    )(trial_sets.transpose(1, 0, 2), tile_pattern[0, 0], tile_count, tile_values[0, 0])
    return out.transpose(1, 0, 2)


def solution(mesh):
    return jax.shard_map(
        local,
        mesh=mesh,
        in_specs=(
            P(None, None, "diag"),
            P("diag", "tri", None, None, None),
            P("diag", "tri", None, None),
            P("diag", "tri"),
        ),
        out_specs=P(None, None, ("diag", "tri")),
        check_vma=False,
    )
```

```python
import functools

import jax
import jax.numpy as jnp
from jax import lax
from jax.experimental import pallas as pl
from jax.experimental.pallas import tpu as pltpu
from jax.sharding import PartitionSpec as P

MESH = pl.DeviceIdType.MESH
UNROLL = 32
CHUNKS = 8


HALVES = (0x2822, 0x8A23, 0x08AB, 0x23AE)


def half_of(i, z_hi, x):
    bits = jnp.where(x < 2, jnp.where(x == 0, HALVES[0], HALVES[1]), jnp.where(x == 2, HALVES[2], HALVES[3]))
    return (bits >> ((i & 7) * 2 + z_hi)) & 1


def tables(pattern, live, place_first):
    rows, cols = pattern[0:1, :], pattern[1:2, :]
    target, source = (rows, cols) if place_first else (cols, rows)
    lane = lax.broadcasted_iota(jnp.int32, (1, 256), 1)
    word = target * 8192 + source * 256 + lane
    word = word + jnp.where(lane < live, 0, 1 << 18)
    word = jnp.where(lane < 192, word, (1 << 20) + lane)

    def column(row):
        wide = jnp.broadcast_to(row, (128, 256))
        tall = jnp.concatenate([wide[:, :128].T, wide[:, 128:].T], 0)
        return jnp.concatenate([tall, tall], 1)

    tall = column(word)
    rank = jnp.sum(jnp.where(tall < word, 1, 0), axis=0, keepdims=True)
    spot = column(rank)
    order = jnp.sum(jnp.where(spot == lane, tall, 0), axis=0, keepdims=True)
    below = jnp.sum(jnp.where(tall < (lane + 1) * 8192, 1, 0), axis=0, keepdims=True)
    before = jnp.sum(jnp.where(tall < lane * 8192, 1, 0), axis=0, keepdims=True)
    ends = jnp.where(below == before, 192, below - 1)
    return order, ends


def coded(values):
    most = functools.reduce(jnp.maximum, [jnp.abs(v) for v in values])
    scale = jnp.maximum(jnp.max(most, axis=1, keepdims=True), 4e-34)
    grow = jnp.broadcast_to(32767.0 / scale, most.shape)
    return [jnp.round(v * grow).astype(jnp.int32).astype(jnp.int16) for v in values], scale * (1 / 32767.0)


def visit(transposed, row, first, last, acc, table, tiles, xs, runs, meet=None):
    contract = (((1,), (1,)), ((), ())) if transposed else (((1,), (0,)), ((), ()))
    side = 0 if transposed else 1

    def body(step, acc):
        if meet:
            meet(step)
        base = step * UNROLL
        words = [table[row, base + u] for u in range(UNROLL)]
        terms = []
        for u in range(0, UNROLL, 2):
            pair = words[u : u + 2]
            left = jnp.concatenate([xs[(w >> 8) & 31] for w in pair], 0)
            right = jnp.concatenate([tiles[w & 255] for w in pair], side)
            both = lax.dot_general(left, right, contract, preferred_element_type=jnp.float32)
            terms += [both[0:24, 0:128], both[24:48, 128:256]]
        past = table[row, jnp.maximum(base - 1, 0)]
        for u in range(UNROLL):
            same = (words[u] >> 13) == (past >> 13)
            past = words[u]
            acc = terms[u] + jnp.where(same, acc, 0.0)
            runs[base + u] = acc
        return acc

    return lax.fori_loop(first, last, body, acc)


def kernel(
    x_hbm, pattern_hbm, count, tiles_hbm, out_ref,
    raw, pattern, padded, table_v, table, tiles, own, held, runs,
    col, col_scale, row, col_got, scale_got, pieces,
    load, tile_sem, x_send, x_recv, col_send, col_recv, scale_send, scale_recv, row_send, row_recv,
):
    i, k = lax.axis_index("diag"), lax.axis_index("tri")
    x, z_hi = k & 3, k >> 2
    source = (i - k) & 31
    home = k == 0
    from_half = half_of(i, z_hi, x)
    giver = {"diag": source, "tri": from_half * 4 + x}
    takers = []
    for h in (0, 1):
        user = (i + 4 * h + x) & 31
        takes = (half_of(user, h, x) == z_hi) & jnp.logical_not((h * 4 + x) == 0)
        takers.append((takes, {"diag": user, "tri": h * 4 + x}))
    peers = [((1 - z_hi) * 4 + ((x + d) & 3)) for d in (2, 1, 3, 0)] + [z_hi * 4 + ((x + d) & 3) for d in (2, 1, 3)]

    get_pattern = pltpu.make_async_copy(pattern_hbm, pattern, load.at[0])
    get_x = pltpu.make_async_copy(x_hbm, raw, load.at[1])
    get_pattern.start()
    get_x.start()
    each = 192 // CHUNKS
    get_tiles = []
    for n in range(CHUNKS):
        part = pl.ds(n * each, each)
        get_tiles.append(pltpu.make_async_copy(tiles_hbm.at[part], tiles.at[part], tile_sem.at[n]))
        get_tiles[n].start()

    barrier = pltpu.get_barrier_semaphore()
    expected = jnp.int32(7)
    for takes, user in [*takers, (jnp.logical_not(home), giver)]:
        expected = expected + takes.astype(jnp.int32)

        @pl.when(takes)
        def _():
            pl.semaphore_signal(barrier, inc=1, device_id=user, device_id_type=MESH)
    for peer in peers:
        pl.semaphore_signal(barrier, inc=1, device_id={"diag": i, "tri": peer}, device_id_type=MESH)

    get_x.wait()
    whole = jnp.concatenate([raw[p] for p in range(12)], 0)
    for c in range(32):
        own[c] = whole[:, c * 128 : (c + 1) * 128]
    get_pattern.wait()
    padded[:, 0:192] = pattern[...]
    padded[:, 192:256] = jnp.zeros((2, 64), jnp.int32)
    pairs = padded[...]
    live = count[0, 0]
    col_order, col_ends = tables(pairs, live, False)
    row_order, row_ends = tables(pairs, live, True)
    table_v[...] = jnp.concatenate([col_order, col_ends, row_order, row_ends] * 2, 0)
    runs[192] = jnp.zeros((24, 128), jnp.float32)
    col_got[2] = jnp.zeros((32, 24, 128), jnp.int16)
    scale_got[2] = jnp.zeros((24, 128), jnp.float32)

    get_table = pltpu.make_async_copy(table_v, table, load.at[2])
    get_table.start()
    get_table.wait()

    for copy in get_tiles:
        copy.wait()
    acc = jnp.zeros((24, 128), jnp.float32)
    meeting = jnp.where(z_hi == 0, jnp.maximum(2 - ((i >> 1) & 3), 0), 0)
    give = []
    for h in (0, 1):
        takes, user = takers[h]
        give.append(
            pltpu.make_async_remote_copy(own, held, x_send.at[h], x_recv, device_id=user, device_id_type=MESH)
        )
    keep = pltpu.make_async_copy(own, held, x_recv)

    def meet(step):
        @pl.when(step == meeting)
        def _():
            pl.semaphore_wait(barrier, expected)
            for h in (0, 1):
                pl.when(takers[h][0])(give[h].start)
            pl.when(home)(keep.start)

    visit(False, 0, 0, 192 // UNROLL, acc, table, tiles, own, runs, meet)
    lane = lax.broadcasted_iota(jnp.int32, (24, 128), 1)
    scales = jnp.zeros((24, 128), jnp.float32)
    for t in range(8):
        codes, scale = coded([runs[table[1, t * 4 + j]] for j in range(4)])
        for j in range(4):
            col[t * 4 + j] = codes[j]
        scales = jnp.where(lane == t, scale, scales)
    col_scale[...] = scales

    back = [
        pltpu.make_async_remote_copy(
            col, col_got.at[z_hi], col_send, col_recv.at[z_hi], device_id=giver, device_id_type=MESH
        ),
        pltpu.make_async_remote_copy(
            col_scale, scale_got.at[z_hi], scale_send, scale_recv.at[z_hi], device_id=giver, device_id_type=MESH
        ),
    ]

    @pl.when(jnp.logical_not(home))
    def _():
        for copy in back:
            copy.start()
        pltpu.make_async_remote_copy(own, held, x_send.at[0], x_recv, device_id=giver, device_id_type=MESH).wait_recv()

    keep_col = pltpu.make_async_copy(col, col_got.at[0], col_recv.at[0])
    keep_scale = pltpu.make_async_copy(col_scale, scale_got.at[0], scale_recv.at[0])

    @pl.when(home)
    def _():
        keep_col.start()
        keep_scale.start()
        keep.wait()

    visit(True, 2, 0, 192 // UNROLL, acc, table, tiles, held, runs)
    @pl.when(home)
    def _():
        keep_col.wait()
        keep_scale.wait()

    slots = []
    for h in (0, 1):
        takes, user = takers[h]
        filled = takes if h else takes | home
        slots.append(jnp.where(filled, h, 2))

        @pl.when(takes)
        def _():
            pltpu.make_async_remote_copy(
                col, col_got.at[h], col_send, col_recv.at[h], device_id=user, device_id_type=MESH
            ).wait_recv()
            pltpu.make_async_remote_copy(
                col_scale, scale_got.at[h], scale_send, scale_recv.at[h], device_id=user, device_id_type=MESH
            ).wait_recv()

    scatter = []
    scales = [scale_got[slot] for slot in slots]
    for n, peer in enumerate([*peers, k]):
        part = [jnp.sum(jnp.where(lane == peer, s, 0.0), axis=1, keepdims=True) for s in scales]
        part = [jnp.broadcast_to(s, (24, 128)) for s in part]
        for j in range(4):
            p = peer * 4 + j
            total = runs[table[3, p]]
            for slot, scale in zip(slots, part):
                total = total + col_got[slot, p].astype(jnp.int32).astype(jnp.float32) * scale
            row[p] = total
        if n == 7:
            break
        copy = pltpu.make_async_remote_copy(
            row.at[pl.ds(peer * 4, 4)],
            pieces.at[n],
            row_send.at[n],
            row_recv.at[n],
            device_id={"diag": i, "tri": peer},
            device_id_type=MESH,
        )
        copy.start()
        scatter.append(copy)

    for h in (0, 1):
        takes, user = takers[h]

        @pl.when(takes)
        def _():
            give[h].wait_send()

    @pl.when(jnp.logical_not(home))
    def _():
        for copy in back:
            copy.wait_send()

    for copy in scatter:
        copy.wait()
    for j in range(4):
        total = row[k * 4 + j]
        for n in range(7):
            total = total + pieces[n, j]
        for p in range(12):
            out_ref[p, :, j * 128 : (j + 1) * 128] = total[2 * p : 2 * p + 2, :]


def local(trial_sets, tile_values, tile_pattern, tile_count):
    sets, vecs, rows = trial_sets.shape
    tri = lax.axis_size("tri")
    columns = sets * vecs
    slots, size = tile_values.shape[2:4]
    blocks = rows // size
    f32, bf16, i32 = jnp.float32, jnp.bfloat16, jnp.int32
    dma = pltpu.SemaphoreType.DMA
    block = (columns, size)
    out = pl.pallas_call(
        kernel,
        out_shape=jax.ShapeDtypeStruct((vecs, sets, rows // tri), f32),
        in_specs=[
            pl.BlockSpec(memory_space=pl.ANY),
            pl.BlockSpec(memory_space=pl.ANY),
            pl.BlockSpec(memory_space=pltpu.SMEM),
            pl.BlockSpec(memory_space=pl.ANY),
        ],
        out_specs=pl.BlockSpec(memory_space=pltpu.VMEM),
        scratch_shapes=[
            pltpu.VMEM((vecs, sets, rows), bf16),
            pltpu.VMEM((2, slots), i32),
            pltpu.VMEM((2, 256), i32),
            pltpu.VMEM((8, 256), i32),
            pltpu.SMEM((8, 256), i32),
            pltpu.VMEM((slots, size, size), bf16),
            pltpu.VMEM((blocks, *block), bf16),
            pltpu.VMEM((blocks, *block), bf16),
            pltpu.VMEM((slots + 8, *block), f32),
            pltpu.VMEM((blocks, *block), jnp.int16),
            pltpu.VMEM(block, f32),
            pltpu.VMEM((blocks, *block), f32),
            pltpu.VMEM((3, blocks, *block), jnp.int16),
            pltpu.VMEM((3, *block), f32),
            pltpu.VMEM((7, 4, *block), f32),
            dma((3,)),
            dma((CHUNKS,)),
            dma((2,)),
            dma(()),
            dma(()),
            dma((2,)),
            dma(()),
            dma((2,)),
            dma((7,)),
            dma((7,)),
        ],
        compiler_params=pltpu.CompilerParams(
            collective_id=0, has_side_effects=True, vmem_limit_bytes=63 << 20
        ),
        name="block_products",
    )(trial_sets.transpose(1, 0, 2), tile_pattern[0, 0], tile_count, tile_values[0, 0])
    return out.transpose(1, 0, 2)


def solution(mesh):
    return jax.shard_map(
        local,
        mesh=mesh,
        in_specs=(
            P(None, None, "diag"),
            P("diag", "tri", None, None, None),
            P("diag", "tri", None, None),
            P("diag", "tri"),
        ),
        out_specs=P(None, None, ("diag", "tri")),
        check_vma=False,
    )
```

```python
import functools

import jax
import jax.numpy as jnp
from jax import lax
from jax.experimental import pallas as pl
from jax.experimental.pallas import tpu as pltpu
from jax.sharding import PartitionSpec as P

MESH = pl.DeviceIdType.MESH
COL_UNROLL = 32
ROW_UNROLL = 48
CHUNKS = 8


HALVES = (0x2822, 0x8A23, 0x08AB, 0x23AE)


def half_of(i, z_hi, x):
    bits = jnp.where(x < 2, jnp.where(x == 0, HALVES[0], HALVES[1]), jnp.where(x == 2, HALVES[2], HALVES[3]))
    return (bits >> ((i & 7) * 2 + z_hi)) & 1


def tables(pattern, live, place_first):
    rows, cols = pattern[0:1, :], pattern[1:2, :]
    target, source = (rows, cols) if place_first else (cols, rows)
    lane = lax.broadcasted_iota(jnp.int32, (1, 256), 1)
    word = target * 8192 + source * 256 + lane
    word = word + jnp.where(lane < live, 0, 1 << 18)
    word = jnp.where(lane < 192, word, (1 << 20) + lane)

    def column(row):
        wide = jnp.broadcast_to(row, (128, 256))
        tall = jnp.concatenate([wide[:, :128].T, wide[:, 128:].T], 0)
        return jnp.concatenate([tall, tall], 1)

    tall = column(word)
    rank = jnp.sum(jnp.where(tall < word, 1, 0), axis=0, keepdims=True)
    spot = column(rank)
    order = jnp.sum(jnp.where(spot == lane, tall, 0), axis=0, keepdims=True)
    below = jnp.sum(jnp.where(tall < (lane + 1) * 8192, 1, 0), axis=0, keepdims=True)
    before = jnp.sum(jnp.where(tall < lane * 8192, 1, 0), axis=0, keepdims=True)
    ends = jnp.where(below == before, 192, below - 1)
    return order, ends


def coded(values):
    most = functools.reduce(jnp.maximum, [jnp.abs(v) for v in values])
    scale = jnp.maximum(jnp.max(most, axis=1, keepdims=True), 4e-34)
    grow = jnp.broadcast_to(32767.0 / scale, most.shape)
    return [jnp.round(v * grow).astype(jnp.int32).astype(jnp.int16) for v in values], scale * (1 / 32767.0)


def packed(values):
    most = functools.reduce(jnp.maximum, [jnp.abs(v) for v in values])
    scale = jnp.maximum(jnp.max(most, axis=1, keepdims=True), 4e-34)
    level = jnp.broadcast_to(jnp.ceil(jnp.log2(scale) * 128.0), most.shape)
    grow = 32700.0 / jnp.exp2(level * (1 / 128.0))
    return [v.astype(jnp.int32).astype(jnp.int16) for v in [*(jnp.round(v * grow) for v in values), level]]


def unpacked(codes):
    scale = jnp.exp2(codes[4].astype(jnp.int32).astype(jnp.float32) * (1 / 128.0)) * (1 / 32700.0)
    return [codes[j].astype(jnp.int32).astype(jnp.float32) * scale for j in range(4)]


def visit(transposed, row, first, last, acc, table, tiles, xs, runs, meet=None):
    contract = (((1,), (1,)), ((), ())) if transposed else (((1,), (0,)), ((), ()))
    side = 0 if transposed else 1
    UNROLL = ROW_UNROLL if transposed else COL_UNROLL

    def body(step, acc):
        if meet:
            meet(step)
        base = step * UNROLL
        words = [table[row, base + u] for u in range(UNROLL)]
        terms = []
        for u in range(0, UNROLL, 2):
            pair = words[u : u + 2]
            left = jnp.concatenate([xs[(w >> 8) & 31] for w in pair], 0)
            right = jnp.concatenate([tiles[w & 255] for w in pair], side)
            both = lax.dot_general(left, right, contract, preferred_element_type=jnp.float32)
            terms += [both[0:24, 0:128], both[24:48, 128:256]]
        past = table[row, jnp.maximum(base - 1, 0)]
        for u in range(UNROLL):
            same = (words[u] >> 13) == (past >> 13)
            past = words[u]
            acc = terms[u] + jnp.where(same, acc, 0.0)
            runs[base + u] = acc
        return acc

    return lax.fori_loop(first, last, body, acc)


def kernel(
    x_hbm, pattern_hbm, count, tiles_hbm, out_ref,
    raw, pattern, padded, table_v, table, tiles, own, held, runs,
    col, col_scale, row, leaving, col_got, scale_got, pieces,
    load, tile_sem, x_send, x_recv, col_send, col_recv, scale_send, scale_recv, row_send, row_recv,
):
    i, k = lax.axis_index("diag"), lax.axis_index("tri")
    x, z_hi = k & 3, k >> 2
    source = (i - k) & 31
    home = k == 0
    from_half = half_of(i, z_hi, x)
    giver = {"diag": source, "tri": from_half * 4 + x}
    takers = []
    for h in (0, 1):
        user = (i + 4 * h + x) & 31
        takes = (half_of(user, h, x) == z_hi) & jnp.logical_not((h * 4 + x) == 0)
        takers.append((takes, {"diag": user, "tri": h * 4 + x}))
    peers = [((1 - z_hi) * 4 + ((x + d) & 3)) for d in (2, 1, 3, 0)] + [z_hi * 4 + ((x + d) & 3) for d in (2, 1, 3)]

    get_pattern = pltpu.make_async_copy(pattern_hbm, pattern, load.at[0])
    get_x = pltpu.make_async_copy(x_hbm, raw, load.at[1])
    get_pattern.start()
    get_x.start()
    each = 192 // CHUNKS
    get_tiles = []
    for n in range(CHUNKS):
        part = pl.ds(n * each, each)
        get_tiles.append(pltpu.make_async_copy(tiles_hbm.at[part], tiles.at[part], tile_sem.at[n]))
        get_tiles[n].start()

    barrier = pltpu.get_barrier_semaphore()
    expected = jnp.int32(7)
    for takes, user in [*takers, (jnp.logical_not(home), giver)]:
        expected = expected + takes.astype(jnp.int32)

        @pl.when(takes)
        def _():
            pl.semaphore_signal(barrier, inc=1, device_id=user, device_id_type=MESH)
    for peer in peers:
        pl.semaphore_signal(barrier, inc=1, device_id={"diag": i, "tri": peer}, device_id_type=MESH)

    get_x.wait()
    whole = jnp.concatenate([raw[p] for p in range(12)], 0)
    for c in range(32):
        own[c] = whole[:, c * 128 : (c + 1) * 128]
    get_pattern.wait()
    padded[:, 0:192] = pattern[...]
    padded[:, 192:256] = jnp.zeros((2, 64), jnp.int32)
    pairs = padded[...]
    live = count[0, 0]
    col_order, col_ends = tables(pairs, live, False)
    row_order, row_ends = tables(pairs, live, True)
    table_v[...] = jnp.concatenate([col_order, col_ends, row_order, row_ends] * 2, 0)
    runs[192] = jnp.zeros((24, 128), jnp.float32)
    col_got[2] = jnp.zeros((32, 24, 128), jnp.int16)
    scale_got[2] = jnp.zeros((24, 128), jnp.float32)

    get_table = pltpu.make_async_copy(table_v, table, load.at[2])
    get_table.start()
    get_table.wait()

    for copy in get_tiles:
        copy.wait()
    acc = jnp.zeros((24, 128), jnp.float32)
    meeting = jnp.where(z_hi == 0, jnp.maximum(2 - ((i >> 1) & 3), 0), 0)
    give = []
    for h in (0, 1):
        takes, user = takers[h]
        give.append(
            pltpu.make_async_remote_copy(own, held, x_send.at[h], x_recv, device_id=user, device_id_type=MESH)
        )
    keep = pltpu.make_async_copy(own, held, x_recv)

    def meet(step):
        @pl.when(step == meeting)
        def _():
            pl.semaphore_wait(barrier, expected)
            for h in (0, 1):
                pl.when(takers[h][0])(give[h].start)
            pl.when(home)(keep.start)

    visit(False, 0, 0, 192 // COL_UNROLL, acc, table, tiles, own, runs, meet)
    lane = lax.broadcasted_iota(jnp.int32, (24, 128), 1)
    scales = jnp.zeros((24, 128), jnp.float32)
    for t in range(8):
        codes, scale = coded([runs[table[1, t * 4 + j]] for j in range(4)])
        for j in range(4):
            col[t * 4 + j] = codes[j]
        scales = jnp.where(lane == t, scale, scales)
    col_scale[...] = scales

    back = [
        pltpu.make_async_remote_copy(
            col, col_got.at[z_hi], col_send, col_recv.at[z_hi], device_id=giver, device_id_type=MESH
        ),
        pltpu.make_async_remote_copy(
            col_scale, scale_got.at[z_hi], scale_send, scale_recv.at[z_hi], device_id=giver, device_id_type=MESH
        ),
    ]

    @pl.when(jnp.logical_not(home))
    def _():
        for copy in back:
            copy.start()
        pltpu.make_async_remote_copy(own, held, x_send.at[0], x_recv, device_id=giver, device_id_type=MESH).wait_recv()

    keep_col = pltpu.make_async_copy(col, col_got.at[0], col_recv.at[0])
    keep_scale = pltpu.make_async_copy(col_scale, scale_got.at[0], scale_recv.at[0])

    @pl.when(home)
    def _():
        keep_col.start()
        keep_scale.start()
        keep.wait()

    visit(True, 2, 0, 192 // ROW_UNROLL, acc, table, tiles, held, runs)
    @pl.when(home)
    def _():
        keep_col.wait()
        keep_scale.wait()

    slots = []
    for h in (0, 1):
        takes, user = takers[h]
        filled = takes if h else takes | home
        slots.append(jnp.where(filled, h, 2))

        @pl.when(takes)
        def _():
            pltpu.make_async_remote_copy(
                col, col_got.at[h], col_send, col_recv.at[h], device_id=user, device_id_type=MESH
            ).wait_recv()
            pltpu.make_async_remote_copy(
                col_scale, scale_got.at[h], scale_send, scale_recv.at[h], device_id=user, device_id_type=MESH
            ).wait_recv()

    scatter = []
    scales = [scale_got[slot] for slot in slots]
    for n, peer in enumerate([*peers, k]):
        part = [jnp.sum(jnp.where(lane == peer, s, 0.0), axis=1, keepdims=True) for s in scales]
        part = [jnp.broadcast_to(s, (24, 128)) for s in part]
        totals = []
        for j in range(4):
            p = peer * 4 + j
            total = runs[table[3, p]]
            for slot, scale in zip(slots, part):
                total = total + col_got[slot, p].astype(jnp.int32).astype(jnp.float32) * scale
            totals.append(total)
        if n == 7:
            for j in range(4):
                row[j] = totals[j]
            break
        for j, codes in enumerate(packed(totals)):
            leaving[n, j] = codes
        copy = pltpu.make_async_remote_copy(
            leaving.at[n],
            pieces.at[n],
            row_send.at[n],
            row_recv.at[n],
            device_id={"diag": i, "tri": peer},
            device_id_type=MESH,
        )
        copy.start()
        scatter.append(copy)

    for h in (0, 1):
        takes, user = takers[h]

        @pl.when(takes)
        def _():
            give[h].wait_send()

    @pl.when(jnp.logical_not(home))
    def _():
        for copy in back:
            copy.wait_send()

    for copy in scatter:
        copy.wait()
    totals = [row[j] for j in range(4)]
    for n in range(7):
        totals = [a + b for a, b in zip(totals, unpacked(pieces.at[n]))]
    for j, total in enumerate(totals):
        for p in range(12):
            out_ref[p, :, j * 128 : (j + 1) * 128] = total[2 * p : 2 * p + 2, :]


def local(trial_sets, tile_values, tile_pattern, tile_count):
    sets, vecs, rows = trial_sets.shape
    tri = lax.axis_size("tri")
    columns = sets * vecs
    slots, size = tile_values.shape[2:4]
    blocks = rows // size
    f32, bf16, i32 = jnp.float32, jnp.bfloat16, jnp.int32
    dma = pltpu.SemaphoreType.DMA
    block = (columns, size)
    hbm = functools.partial(pltpu.with_memory_space_constraint, memory_space=pltpu.HBM)
    out = pl.pallas_call(
        kernel,
        out_shape=jax.ShapeDtypeStruct((vecs, sets, rows // tri), f32),
        in_specs=[
            pl.BlockSpec(memory_space=pltpu.HBM),
            pl.BlockSpec(memory_space=pltpu.HBM),
            pl.BlockSpec(memory_space=pltpu.SMEM),
            pl.BlockSpec(memory_space=pltpu.HBM),
        ],
        out_specs=pl.BlockSpec(memory_space=pltpu.VMEM),
        scratch_shapes=[
            pltpu.VMEM((vecs, sets, rows), bf16),
            pltpu.VMEM((2, slots), i32),
            pltpu.VMEM((2, 256), i32),
            pltpu.VMEM((8, 256), i32),
            pltpu.SMEM((8, 256), i32),
            pltpu.VMEM((slots, size, size), bf16),
            pltpu.VMEM((blocks, *block), bf16),
            pltpu.VMEM((blocks, *block), bf16),
            pltpu.VMEM((slots + 8, *block), f32),
            pltpu.VMEM((blocks, *block), jnp.int16),
            pltpu.VMEM(block, f32),
            pltpu.VMEM((4, *block), f32),
            pltpu.VMEM((7, 5, *block), jnp.int16),
            pltpu.VMEM((3, blocks, *block), jnp.int16),
            pltpu.VMEM((3, *block), f32),
            pltpu.VMEM((7, 5, *block), jnp.int16),
            dma((3,)),
            dma((CHUNKS,)),
            dma((2,)),
            dma(()),
            dma(()),
            dma((2,)),
            dma(()),
            dma((2,)),
            dma((7,)),
            dma((7,)),
        ],
        compiler_params=pltpu.CompilerParams(
            collective_id=0, has_side_effects=True, vmem_limit_bytes=40 << 20
        ),
        name="block_products",
    )(hbm(trial_sets.transpose(1, 0, 2)), hbm(tile_pattern[0, 0]), tile_count, hbm(tile_values[0, 0]))
    return out.transpose(1, 0, 2)


def solution(mesh):
    return jax.shard_map(
        local,
        mesh=mesh,
        in_specs=(
            P(None, None, "diag"),
            P("diag", "tri", None, None, None),
            P("diag", "tri", None, None),
            P("diag", "tri"),
        ),
        out_specs=P(None, None, ("diag", "tri")),
        check_vma=False,
    )
```

```python
import functools

import jax
import jax.numpy as jnp
from jax import lax
from jax.experimental import pallas as pl
from jax.experimental.pallas import tpu as pltpu
from jax.sharding import PartitionSpec as P

MESH = pl.DeviceIdType.MESH
COL_UNROLL = 32
MEETINGS = 0o10000123
ROW_UNROLL = 48
CHUNKS = 8


HALVES = (0x2822, 0x8A23, 0x08AB, 0x23AE)


def half_of(i, z_hi, x):
    bits = jnp.where(x < 2, jnp.where(x == 0, HALVES[0], HALVES[1]), jnp.where(x == 2, HALVES[2], HALVES[3]))
    return (bits >> ((i & 7) * 2 + z_hi)) & 1


def tables(pattern, live, place_first):
    rows, cols = pattern[0:1, :], pattern[1:2, :]
    target, source = (rows, cols) if place_first else (cols, rows)
    lane = lax.broadcasted_iota(jnp.int32, (1, 256), 1)
    word = target * 8192 + source * 256 + lane
    word = word + jnp.where(lane < live, 0, 1 << 18)
    word = jnp.where(lane < 192, word, (1 << 20) + lane)

    def column(row):
        wide = jnp.broadcast_to(row, (128, 256))
        tall = jnp.concatenate([wide[:, :128].T, wide[:, 128:].T], 0)
        return jnp.concatenate([tall, tall], 1)

    tall = column(word)
    rank = jnp.sum(jnp.where(tall < word, 1, 0), axis=0, keepdims=True)
    spot = column(rank)
    order = jnp.sum(jnp.where(spot == lane, tall, 0), axis=0, keepdims=True)
    below = jnp.sum(jnp.where(tall < (lane + 1) * 8192, 1, 0), axis=0, keepdims=True)
    before = jnp.sum(jnp.where(tall < lane * 8192, 1, 0), axis=0, keepdims=True)
    ends = jnp.where(below == before, 192, below - 1)
    return order, ends


def coded(values):
    most = functools.reduce(jnp.maximum, [jnp.abs(v) for v in values])
    scale = jnp.maximum(jnp.max(most, axis=1, keepdims=True), 4e-34)
    grow = jnp.broadcast_to(32767.0 / scale, most.shape)
    return [jnp.round(v * grow).astype(jnp.int32).astype(jnp.int16) for v in values], scale * (1 / 32767.0)


def packed(values):
    most = functools.reduce(jnp.maximum, [jnp.abs(v) for v in values])
    scale = jnp.maximum(jnp.max(most, axis=1, keepdims=True), 4e-34)
    level = jnp.broadcast_to(jnp.ceil(jnp.log2(scale) * 128.0), most.shape)
    grow = 32700.0 / jnp.exp2(level * (1 / 128.0))
    return [v.astype(jnp.int32).astype(jnp.int16) for v in [*(jnp.round(v * grow) for v in values), level]]


def unpacked(codes):
    scale = jnp.exp2(codes[4].astype(jnp.int32).astype(jnp.float32) * (1 / 128.0)) * (1 / 32700.0)
    return [codes[j].astype(jnp.int32).astype(jnp.float32) * scale for j in range(4)]


def visit(transposed, row, first, last, acc, table, tiles, xs, runs, meet=None):
    contract = (((1,), (1,)), ((), ())) if transposed else (((1,), (0,)), ((), ()))
    side = 0 if transposed else 1
    UNROLL = ROW_UNROLL if transposed else COL_UNROLL

    def body(step, acc):
        if meet:
            meet(step)
        base = step * UNROLL
        words = [table[row, base + u] for u in range(UNROLL)]
        terms = []
        for u in range(0, UNROLL, 2):
            pair = words[u : u + 2]
            left = jnp.concatenate([xs[(w >> 8) & 31] for w in pair], 0)
            right = jnp.concatenate([tiles[w & 255] for w in pair], side)
            both = lax.dot_general(left, right, contract, preferred_element_type=jnp.float32)
            terms += [both[0:24, 0:128], both[24:48, 128:256]]
        past = table[row, jnp.maximum(base - 1, 0)]
        for u in range(UNROLL):
            same = (words[u] >> 13) == (past >> 13)
            past = words[u]
            acc = terms[u] + jnp.where(same, acc, 0.0)
            runs[base + u] = acc
        return acc

    return lax.fori_loop(first, last, body, acc)


def kernel(
    x_hbm, pattern_hbm, count, tiles_hbm, out_ref,
    raw, pattern, padded, table_v, table, tiles, own, held, runs,
    col, col_scale, row, leaving, col_got, scale_got, pieces,
    load, tile_sem, x_send, x_recv, col_send, col_recv, scale_send, scale_recv, row_send, row_recv,
):
    i, k = lax.axis_index("diag"), lax.axis_index("tri")
    x, z_hi = k & 3, k >> 2
    source = (i - k) & 31
    home = k == 0
    from_half = half_of(i, z_hi, x)
    giver = {"diag": source, "tri": from_half * 4 + x}
    takers = []
    for h in (0, 1):
        user = (i + 4 * h + x) & 31
        takes = (half_of(user, h, x) == z_hi) & jnp.logical_not((h * 4 + x) == 0)
        takers.append((takes, {"diag": user, "tri": h * 4 + x}))
    peers = [((1 - z_hi) * 4 + ((x + d) & 3)) for d in (2, 1, 3, 0)] + [z_hi * 4 + ((x + d) & 3) for d in (2, 1, 3)]

    get_pattern = pltpu.make_async_copy(pattern_hbm, pattern, load.at[0])
    get_x = pltpu.make_async_copy(x_hbm, raw, load.at[1])
    get_pattern.start()
    get_x.start()
    each = 192 // CHUNKS
    get_tiles = []
    for n in range(CHUNKS):
        part = pl.ds(n * each, each)
        get_tiles.append(pltpu.make_async_copy(tiles_hbm.at[part], tiles.at[part], tile_sem.at[n]))
        get_tiles[n].start()

    barrier = pltpu.get_barrier_semaphore()
    expected = jnp.int32(7)
    for takes, user in [*takers, (jnp.logical_not(home), giver)]:
        expected = expected + takes.astype(jnp.int32)

        @pl.when(takes)
        def _():
            pl.semaphore_signal(barrier, inc=1, device_id=user, device_id_type=MESH)
    for peer in peers:
        pl.semaphore_signal(barrier, inc=1, device_id={"diag": i, "tri": peer}, device_id_type=MESH)

    get_x.wait()
    whole = jnp.concatenate([raw[p] for p in range(12)], 0)
    for c in range(32):
        own[c] = whole[:, c * 128 : (c + 1) * 128]
    meeting = ((MEETINGS >> (3 * (((i >> 1) & 3) + 4 * z_hi))) & 7) - 1
    give = []
    for h in (0, 1):
        takes, user = takers[h]
        give.append(
            pltpu.make_async_remote_copy(own, held, x_send.at[h], x_recv, device_id=user, device_id_type=MESH)
        )
    keep = pltpu.make_async_copy(own, held, x_recv)

    def meet(step):
        @pl.when(step == meeting)
        def _():
            pl.semaphore_wait(barrier, expected)
            for h in (0, 1):
                pl.when(takers[h][0])(give[h].start)
            pl.when(home)(keep.start)

    meet(-1)
    get_pattern.wait()
    padded[:, 0:192] = pattern[...]
    padded[:, 192:256] = jnp.zeros((2, 64), jnp.int32)
    pairs = padded[...]
    live = count[0, 0]
    col_order, col_ends = tables(pairs, live, False)
    row_order, row_ends = tables(pairs, live, True)
    table_v[...] = jnp.concatenate([col_order, col_ends, row_order, row_ends] * 2, 0)
    runs[192] = jnp.zeros((24, 128), jnp.float32)
    col_got[2] = jnp.zeros((32, 24, 128), jnp.int16)
    scale_got[2] = jnp.zeros((24, 128), jnp.float32)

    get_table = pltpu.make_async_copy(table_v, table, load.at[2])
    get_table.start()
    get_table.wait()

    for copy in get_tiles:
        copy.wait()
    acc = jnp.zeros((24, 128), jnp.float32)
    visit(False, 0, 0, 192 // COL_UNROLL, acc, table, tiles, own, runs, meet)
    lane = lax.broadcasted_iota(jnp.int32, (24, 128), 1)
    scales = jnp.zeros((24, 128), jnp.float32)
    for t in range(8):
        codes, scale = coded([runs[table[1, t * 4 + j]] for j in range(4)])
        for j in range(4):
            col[t * 4 + j] = codes[j]
        scales = jnp.where(lane == t, scale, scales)
    col_scale[...] = scales

    back = [
        pltpu.make_async_remote_copy(
            col, col_got.at[z_hi], col_send, col_recv.at[z_hi], device_id=giver, device_id_type=MESH
        ),
        pltpu.make_async_remote_copy(
            col_scale, scale_got.at[z_hi], scale_send, scale_recv.at[z_hi], device_id=giver, device_id_type=MESH
        ),
    ]

    @pl.when(jnp.logical_not(home))
    def _():
        for copy in back:
            copy.start()
        pltpu.make_async_remote_copy(own, held, x_send.at[0], x_recv, device_id=giver, device_id_type=MESH).wait_recv()

    keep_col = pltpu.make_async_copy(col, col_got.at[0], col_recv.at[0])
    keep_scale = pltpu.make_async_copy(col_scale, scale_got.at[0], scale_recv.at[0])

    @pl.when(home)
    def _():
        keep_col.start()
        keep_scale.start()
        keep.wait()

    visit(True, 2, 0, 192 // ROW_UNROLL, acc, table, tiles, held, runs)
    @pl.when(home)
    def _():
        keep_col.wait()
        keep_scale.wait()

    slots = []
    for h in (0, 1):
        takes, user = takers[h]
        filled = takes if h else takes | home
        slots.append(jnp.where(filled, h, 2))

        @pl.when(takes)
        def _():
            pltpu.make_async_remote_copy(
                col, col_got.at[h], col_send, col_recv.at[h], device_id=user, device_id_type=MESH
            ).wait_recv()
            pltpu.make_async_remote_copy(
                col_scale, scale_got.at[h], scale_send, scale_recv.at[h], device_id=user, device_id_type=MESH
            ).wait_recv()

    scatter = []
    scales = [scale_got[slot] for slot in slots]
    for n, peer in enumerate([*peers, k]):
        part = [jnp.sum(jnp.where(lane == peer, s, 0.0), axis=1, keepdims=True) for s in scales]
        part = [jnp.broadcast_to(s, (24, 128)) for s in part]
        totals = []
        for j in range(4):
            p = peer * 4 + j
            total = runs[table[3, p]]
            for slot, scale in zip(slots, part):
                total = total + col_got[slot, p].astype(jnp.int32).astype(jnp.float32) * scale
            totals.append(total)
        if n == 7:
            for j in range(4):
                row[j] = totals[j]
            break
        for j, codes in enumerate(packed(totals)):
            leaving[n, j] = codes
        copy = pltpu.make_async_remote_copy(
            leaving.at[n],
            pieces.at[n],
            row_send.at[n],
            row_recv.at[n],
            device_id={"diag": i, "tri": peer},
            device_id_type=MESH,
        )
        copy.start()
        scatter.append(copy)

    totals = [row[j] for j in range(4)]
    for n in (4, 5, 6, 3, 0, 1, 2):
        scatter[n].wait_recv()
        totals = [a + b for a, b in zip(totals, unpacked(pieces.at[n]))]
    for j, total in enumerate(totals):
        for p in range(12):
            out_ref[p, :, j * 128 : (j + 1) * 128] = total[2 * p : 2 * p + 2, :]
    for h in (0, 1):
        takes, user = takers[h]

        @pl.when(takes)
        def _():
            give[h].wait_send()

    @pl.when(jnp.logical_not(home))
    def _():
        for copy in back:
            copy.wait_send()
    for copy in scatter:
        copy.wait_send()


def local(trial_sets, tile_values, tile_pattern, tile_count):
    sets, vecs, rows = trial_sets.shape
    tri = lax.axis_size("tri")
    columns = sets * vecs
    slots, size = tile_values.shape[2:4]
    blocks = rows // size
    f32, bf16, i32 = jnp.float32, jnp.bfloat16, jnp.int32
    dma = pltpu.SemaphoreType.DMA
    block = (columns, size)
    hbm = functools.partial(pltpu.with_memory_space_constraint, memory_space=pltpu.HBM)
    out = pl.pallas_call(
        kernel,
        out_shape=jax.ShapeDtypeStruct((vecs, sets, rows // tri), f32),
        in_specs=[
            pl.BlockSpec(memory_space=pltpu.HBM),
            pl.BlockSpec(memory_space=pltpu.HBM),
            pl.BlockSpec(memory_space=pltpu.SMEM),
            pl.BlockSpec(memory_space=pltpu.HBM),
        ],
        out_specs=pl.BlockSpec(memory_space=pltpu.VMEM),
        scratch_shapes=[
            pltpu.VMEM((vecs, sets, rows), bf16),
            pltpu.VMEM((2, slots), i32),
            pltpu.VMEM((2, 256), i32),
            pltpu.VMEM((8, 256), i32),
            pltpu.SMEM((8, 256), i32),
            pltpu.VMEM((slots, size, size), bf16),
            pltpu.VMEM((blocks, *block), bf16),
            pltpu.VMEM((blocks, *block), bf16),
            pltpu.VMEM((slots + 8, *block), f32),
            pltpu.VMEM((blocks, *block), jnp.int16),
            pltpu.VMEM(block, f32),
            pltpu.VMEM((4, *block), f32),
            pltpu.VMEM((7, 5, *block), jnp.int16),
            pltpu.VMEM((3, blocks, *block), jnp.int16),
            pltpu.VMEM((3, *block), f32),
            pltpu.VMEM((7, 5, *block), jnp.int16),
            dma((3,)),
            dma((CHUNKS,)),
            dma((2,)),
            dma(()),
            dma(()),
            dma((2,)),
            dma(()),
            dma((2,)),
            dma((7,)),
            dma((7,)),
        ],
        compiler_params=pltpu.CompilerParams(
            collective_id=0, has_side_effects=True, vmem_limit_bytes=40 << 20
        ),
        name="block_products",
    )(hbm(trial_sets.transpose(1, 0, 2)), hbm(tile_pattern[0, 0]), tile_count, hbm(tile_values[0, 0]))
    return out.transpose(1, 0, 2)


def solution(mesh):
    return jax.shard_map(
        local,
        mesh=mesh,
        in_specs=(
            P(None, None, "diag"),
            P("diag", "tri", None, None, None),
            P("diag", "tri", None, None),
            P("diag", "tri"),
        ),
        out_specs=P(None, None, ("diag", "tri")),
        check_vma=False,
    )
```

```python
import functools

import jax
import jax.numpy as jnp
from jax import lax
from jax.experimental import pallas as pl
from jax.experimental.pallas import tpu as pltpu
from jax.sharding import PartitionSpec as P

MESH = pl.DeviceIdType.MESH
COL_UNROLL = 32
MEETINGS = 0o10000123
ROW_UNROLL = 48
CHUNKS = 8


HALVES = (0x2822, 0x8A23, 0x08AB, 0x23AE)


def half_of(i, z_hi, x):
    bits = jnp.where(x < 2, jnp.where(x == 0, HALVES[0], HALVES[1]), jnp.where(x == 2, HALVES[2], HALVES[3]))
    return (bits >> ((i & 7) * 2 + z_hi)) & 1


def tables(pattern, live, place_first):
    rows, cols = pattern[0:1, :], pattern[1:2, :]
    target, source = (rows, cols) if place_first else (cols, rows)
    lane = lax.broadcasted_iota(jnp.int32, (1, 256), 1)
    word = target * 8192 + source * 256 + lane
    word = word + jnp.where(lane < live, 0, 1 << 18)
    word = jnp.where(lane < 192, word, (1 << 20) + lane)

    def column(row):
        wide = jnp.broadcast_to(row, (128, 256))
        tall = jnp.concatenate([wide[:, :128].T, wide[:, 128:].T], 0)
        return jnp.concatenate([tall, tall], 1)

    tall = column(word)
    rank = jnp.sum(jnp.where(tall < word, 1, 0), axis=0, keepdims=True)
    spot = column(rank)
    order = jnp.sum(jnp.where(spot == lane, tall, 0), axis=0, keepdims=True)
    below = jnp.sum(jnp.where(tall < (lane + 1) * 8192, 1, 0), axis=0, keepdims=True)
    before = jnp.sum(jnp.where(tall < lane * 8192, 1, 0), axis=0, keepdims=True)
    ends = jnp.where(below == before, 192, below - 1)
    return order, ends


def coded(values):
    most = functools.reduce(jnp.maximum, [jnp.abs(v) for v in values])
    scale = jnp.maximum(jnp.max(most, axis=1, keepdims=True), 4e-34)
    grow = jnp.broadcast_to(32767.0 / scale, most.shape)
    return [jnp.round(v * grow).astype(jnp.int32).astype(jnp.int16) for v in values], scale * (1 / 32767.0)


def packed(values):
    most = functools.reduce(jnp.maximum, [jnp.abs(v) for v in values])
    scale = jnp.maximum(jnp.max(most, axis=1, keepdims=True), 4e-34)
    level = jnp.broadcast_to(jnp.ceil(jnp.log2(scale) * 128.0), most.shape)
    grow = 32700.0 / jnp.exp2(level * (1 / 128.0))
    return [v.astype(jnp.int32).astype(jnp.int16) for v in [*(jnp.round(v * grow) for v in values), level]]


def unpacked(codes):
    scale = jnp.exp2(codes[4].astype(jnp.int32).astype(jnp.float32) * (1 / 128.0)) * (1 / 32700.0)
    return [codes[j].astype(jnp.int32).astype(jnp.float32) * scale for j in range(4)]


def visit(transposed, row, first, last, acc, table, tiles, xs, runs, meet=None):
    contract = (((1,), (1,)), ((), ())) if transposed else (((1,), (0,)), ((), ()))
    side = 0 if transposed else 1
    UNROLL = ROW_UNROLL if transposed else COL_UNROLL

    def body(step, acc):
        if meet:
            meet(step)
        base = step * UNROLL
        words = [table[row, base + u] for u in range(UNROLL)]
        terms = []
        for u in range(0, UNROLL, 2):
            pair = words[u : u + 2]
            left = jnp.concatenate([xs[(w >> 8) & 31] for w in pair], 0)
            right = jnp.concatenate([tiles[w & 255] for w in pair], side)
            both = lax.dot_general(left, right, contract, preferred_element_type=jnp.float32)
            terms += [both[0:24, 0:128], both[24:48, 128:256]]
        past = table[row, jnp.maximum(base - 1, 0)]
        for u in range(UNROLL):
            same = (words[u] >> 13) == (past >> 13)
            past = words[u]
            acc = terms[u] + jnp.where(same, acc, 0.0)
            runs[base + u] = acc
        return acc

    return lax.fori_loop(first, last, body, acc)


def kernel(
    x_hbm, pattern_hbm, count, tiles_hbm, out_ref,
    raw, pattern, padded, table_v, table, tiles, own, held, runs,
    col, col_scale, row, leaving, col_got, scale_got, pieces,
    load, tile_sem, x_send, x_recv, col_send, col_recv, scale_send, scale_recv, row_send, row_recv,
):
    i, k = lax.axis_index("diag"), lax.axis_index("tri")
    x, z_hi = k & 3, k >> 2
    source = (i - k) & 31
    home = k == 0
    from_half = half_of(i, z_hi, x)
    giver = {"diag": source, "tri": from_half * 4 + x}
    takers = []
    for h in (0, 1):
        user = (i + 4 * h + x) & 31
        takes = (half_of(user, h, x) == z_hi) & jnp.logical_not((h * 4 + x) == 0)
        takers.append((takes, {"diag": user, "tri": h * 4 + x}))
    peers = [((1 - z_hi) * 4 + ((x + d) & 3)) for d in (2, 3, 1, 0)] + [z_hi * 4 + ((x + d) & 3) for d in (2, 3, 1)]

    get_pattern = pltpu.make_async_copy(pattern_hbm, pattern, load.at[0])
    get_x = pltpu.make_async_copy(x_hbm, raw, load.at[1])
    get_pattern.start()
    get_x.start()
    each = 192 // CHUNKS
    get_tiles = []
    for n in range(CHUNKS):
        part = pl.ds(n * each, each)
        get_tiles.append(pltpu.make_async_copy(tiles_hbm.at[part], tiles.at[part], tile_sem.at[n]))
        get_tiles[n].start()

    barrier = pltpu.get_barrier_semaphore()
    expected = jnp.int32(7)
    for takes, user in [*takers, (jnp.logical_not(home), giver)]:
        expected = expected + takes.astype(jnp.int32)

        @pl.when(takes)
        def _():
            pl.semaphore_signal(barrier, inc=1, device_id=user, device_id_type=MESH)
    for peer in peers:
        pl.semaphore_signal(barrier, inc=1, device_id={"diag": i, "tri": peer}, device_id_type=MESH)

    get_x.wait()
    whole = jnp.concatenate([raw[p] for p in range(12)], 0)
    for c in range(32):
        own[c] = whole[:, c * 128 : (c + 1) * 128]
    meeting = ((MEETINGS >> (3 * (((i >> 1) & 3) + 4 * z_hi))) & 7) - 1
    give = []
    for h in (0, 1):
        takes, user = takers[h]
        give.append(
            pltpu.make_async_remote_copy(own, held, x_send.at[h], x_recv, device_id=user, device_id_type=MESH)
        )
    keep = pltpu.make_async_copy(own, held, x_recv)

    def meet(step):
        @pl.when(step == meeting)
        def _():
            pl.semaphore_wait(barrier, expected)
            for h in (0, 1):
                pl.when(takers[h][0])(give[h].start)
            pl.when(home)(keep.start)

    meet(-1)
    get_pattern.wait()
    padded[:, 0:192] = pattern[...]
    padded[:, 192:256] = jnp.zeros((2, 64), jnp.int32)
    pairs = padded[...]
    live = count[0, 0]
    col_order, col_ends = tables(pairs, live, False)
    row_order, row_ends = tables(pairs, live, True)
    table_v[...] = jnp.concatenate([col_order, col_ends, row_order, row_ends] * 2, 0)
    runs[192] = jnp.zeros((24, 128), jnp.float32)
    col_got[2] = jnp.zeros((32, 24, 128), jnp.int16)
    scale_got[2] = jnp.zeros((24, 128), jnp.float32)

    get_table = pltpu.make_async_copy(table_v, table, load.at[2])
    get_table.start()
    get_table.wait()

    for copy in get_tiles:
        copy.wait()
    acc = jnp.zeros((24, 128), jnp.float32)
    visit(False, 0, 0, 192 // COL_UNROLL, acc, table, tiles, own, runs, meet)
    lane = lax.broadcasted_iota(jnp.int32, (24, 128), 1)
    scales = jnp.zeros((24, 128), jnp.float32)
    for t in range(8):
        codes, scale = coded([runs[table[1, t * 4 + j]] for j in range(4)])
        for j in range(4):
            col[t * 4 + j] = codes[j]
        scales = jnp.where(lane == t, scale, scales)
    col_scale[...] = scales

    back = [
        pltpu.make_async_remote_copy(
            col, col_got.at[z_hi], col_send, col_recv.at[z_hi], device_id=giver, device_id_type=MESH
        ),
        pltpu.make_async_remote_copy(
            col_scale, scale_got.at[z_hi], scale_send, scale_recv.at[z_hi], device_id=giver, device_id_type=MESH
        ),
    ]

    @pl.when(jnp.logical_not(home))
    def _():
        for copy in back:
            copy.start()
        pltpu.make_async_remote_copy(own, held, x_send.at[0], x_recv, device_id=giver, device_id_type=MESH).wait_recv()

    keep_col = pltpu.make_async_copy(col, col_got.at[0], col_recv.at[0])
    keep_scale = pltpu.make_async_copy(col_scale, scale_got.at[0], scale_recv.at[0])

    @pl.when(home)
    def _():
        keep_col.start()
        keep_scale.start()
        keep.wait()

    visit(True, 2, 0, 192 // ROW_UNROLL, acc, table, tiles, held, runs)
    @pl.when(home)
    def _():
        keep_col.wait()
        keep_scale.wait()

    slots = []
    for h in (0, 1):
        takes, user = takers[h]
        filled = takes if h else takes | home
        slots.append(jnp.where(filled, h, 2))

        @pl.when(takes)
        def _():
            pltpu.make_async_remote_copy(
                col, col_got.at[h], col_send, col_recv.at[h], device_id=user, device_id_type=MESH
            ).wait_recv()
            pltpu.make_async_remote_copy(
                col_scale, scale_got.at[h], scale_send, scale_recv.at[h], device_id=user, device_id_type=MESH
            ).wait_recv()

    scatter = []
    scales = [scale_got[slot] for slot in slots]
    for n, peer in enumerate([*peers, k]):
        part = [jnp.sum(jnp.where(lane == peer, s, 0.0), axis=1, keepdims=True) for s in scales]
        part = [jnp.broadcast_to(s, (24, 128)) for s in part]
        totals = []
        for j in range(4):
            p = peer * 4 + j
            total = runs[table[3, p]]
            for slot, scale in zip(slots, part):
                total = total + col_got[slot, p].astype(jnp.int32).astype(jnp.float32) * scale
            totals.append(total)
        if n == 7:
            for j in range(4):
                row[j] = totals[j]
            break
        for j, codes in enumerate(packed(totals)):
            leaving[n, j] = codes
        copy = pltpu.make_async_remote_copy(
            leaving.at[n],
            pieces.at[n],
            row_send.at[n],
            row_recv.at[n],
            device_id={"diag": i, "tri": peer},
            device_id_type=MESH,
        )
        copy.start()
        scatter.append(copy)

    totals = [row[j] for j in range(4)]
    for n in (4, 5, 6, 3, 0, 1, 2):
        scatter[n].wait_recv()
        totals = [a + b for a, b in zip(totals, unpacked(pieces.at[n]))]
    for j, total in enumerate(totals):
        for p in range(12):
            out_ref[p, :, j * 128 : (j + 1) * 128] = total[2 * p : 2 * p + 2, :]
    for h in (0, 1):
        takes, user = takers[h]

        @pl.when(takes)
        def _():
            give[h].wait_send()

    @pl.when(jnp.logical_not(home))
    def _():
        for copy in back:
            copy.wait_send()
    for copy in scatter:
        copy.wait_send()


def local(trial_sets, tile_values, tile_pattern, tile_count):
    sets, vecs, rows = trial_sets.shape
    tri = lax.axis_size("tri")
    columns = sets * vecs
    slots, size = tile_values.shape[2:4]
    blocks = rows // size
    f32, bf16, i32 = jnp.float32, jnp.bfloat16, jnp.int32
    dma = pltpu.SemaphoreType.DMA
    block = (columns, size)
    hbm = functools.partial(pltpu.with_memory_space_constraint, memory_space=pltpu.HBM)
    out = pl.pallas_call(
        kernel,
        out_shape=jax.ShapeDtypeStruct((vecs, sets, rows // tri), f32),
        in_specs=[
            pl.BlockSpec(memory_space=pltpu.HBM),
            pl.BlockSpec(memory_space=pltpu.HBM),
            pl.BlockSpec(memory_space=pltpu.SMEM),
            pl.BlockSpec(memory_space=pltpu.HBM),
        ],
        out_specs=pl.BlockSpec(memory_space=pltpu.VMEM),
        scratch_shapes=[
            pltpu.VMEM((vecs, sets, rows), bf16),
            pltpu.VMEM((2, slots), i32),
            pltpu.VMEM((2, 256), i32),
            pltpu.VMEM((8, 256), i32),
            pltpu.SMEM((8, 256), i32),
            pltpu.VMEM((slots, size, size), bf16),
            pltpu.VMEM((blocks, *block), bf16),
            pltpu.VMEM((blocks, *block), bf16),
            pltpu.VMEM((slots + 8, *block), f32),
            pltpu.VMEM((blocks, *block), jnp.int16),
            pltpu.VMEM(block, f32),
            pltpu.VMEM((4, *block), f32),
            pltpu.VMEM((7, 5, *block), jnp.int16),
            pltpu.VMEM((3, blocks, *block), jnp.int16),
            pltpu.VMEM((3, *block), f32),
            pltpu.VMEM((7, 5, *block), jnp.int16),
            dma((3,)),
            dma((CHUNKS,)),
            dma((2,)),
            dma(()),
            dma(()),
            dma((2,)),
            dma(()),
            dma((2,)),
            dma((7,)),
            dma((7,)),
        ],
        compiler_params=pltpu.CompilerParams(
            collective_id=0, has_side_effects=True, vmem_limit_bytes=40 << 20
        ),
        name="block_products",
    )(hbm(trial_sets.transpose(1, 0, 2)), hbm(tile_pattern[0, 0]), tile_count, hbm(tile_values[0, 0]))
    return out.transpose(1, 0, 2)


def solution(mesh):
    return jax.shard_map(
        local,
        mesh=mesh,
        in_specs=(
            P(None, None, "diag"),
            P("diag", "tri", None, None, None),
            P("diag", "tri", None, None),
            P("diag", "tri"),
        ),
        out_specs=P(None, None, ("diag", "tri")),
        check_vma=False,
    )
```

```python
import functools

import jax
import jax.numpy as jnp
from jax import lax
from jax.experimental import pallas as pl
from jax.experimental.pallas import tpu as pltpu
from jax.sharding import PartitionSpec as P

MESH = pl.DeviceIdType.MESH
COL_UNROLL = 32
MEETINGS = 0o10000123
ROW_UNROLL = 48
CHUNKS = 8


HALVES = (0x2822, 0x8A23, 0x08AB, 0x23AE)


def half_of(i, z_hi, x):
    bits = jnp.where(x < 2, jnp.where(x == 0, HALVES[0], HALVES[1]), jnp.where(x == 2, HALVES[2], HALVES[3]))
    return (bits >> ((i & 7) * 2 + z_hi)) & 1


def tables(pattern, live, place_first):
    rows, cols = pattern[0:1, :], pattern[1:2, :]
    target, source = (rows, cols) if place_first else (cols, rows)
    lane = lax.broadcasted_iota(jnp.int32, (1, 256), 1)
    word = target * 8192 + source * 256 + lane
    word = word + jnp.where(lane < live, 0, 1 << 18)
    word = jnp.where(lane < 192, word, (1 << 20) + lane)

    def column(row):
        wide = jnp.broadcast_to(row, (128, 256))
        tall = jnp.concatenate([wide[:, :128].T, wide[:, 128:].T], 0)
        return jnp.concatenate([tall, tall], 1)

    tall = column(word)
    rank = jnp.sum(jnp.where(tall < word, 1, 0), axis=0, keepdims=True)
    spot = column(rank)
    order = jnp.sum(jnp.where(spot == lane, tall, 0), axis=0, keepdims=True)
    below = jnp.sum(jnp.where(tall < (lane + 1) * 8192, 1, 0), axis=0, keepdims=True)
    before = jnp.sum(jnp.where(tall < lane * 8192, 1, 0), axis=0, keepdims=True)
    ends = jnp.where(below == before, 192, below - 1)
    return order, ends


def coded(values):
    most = functools.reduce(jnp.maximum, [jnp.abs(v) for v in values])
    scale = jnp.maximum(jnp.max(most, axis=1, keepdims=True), 4e-34)
    grow = jnp.broadcast_to(32767.0 / scale, most.shape)
    return [jnp.round(v * grow).astype(jnp.int32).astype(jnp.int16) for v in values], scale * (1 / 32767.0)


def packed(values):
    most = functools.reduce(jnp.maximum, [jnp.abs(v) for v in values])
    scale = jnp.maximum(jnp.max(most, axis=1, keepdims=True), 4e-34)
    level = jnp.broadcast_to(jnp.ceil(jnp.log2(scale) * 128.0), most.shape)
    grow = 32700.0 / jnp.exp2(level * (1 / 128.0))
    return [v.astype(jnp.int32).astype(jnp.int16) for v in [*(jnp.round(v * grow) for v in values), level]]


def unpacked(codes):
    scale = jnp.exp2(codes[4].astype(jnp.int32).astype(jnp.float32) * (1 / 128.0)) * (1 / 32700.0)
    return [codes[j].astype(jnp.int32).astype(jnp.float32) * scale for j in range(4)]


def visit(transposed, row, first, last, acc, table, tiles, xs, runs, meet=None):
    contract = (((1,), (1,)), ((), ())) if transposed else (((1,), (0,)), ((), ()))
    side = 0 if transposed else 1
    UNROLL = ROW_UNROLL if transposed else COL_UNROLL

    def body(step, acc):
        if meet:
            meet(step)
        base = step * UNROLL
        words = [table[row, base + u] for u in range(UNROLL)]
        terms = []
        for u in range(0, UNROLL, 2):
            pair = words[u : u + 2]
            left = jnp.concatenate([xs[(w >> 8) & 31] for w in pair], 0)
            right = jnp.concatenate([tiles[w & 255] for w in pair], side)
            both = lax.dot_general(left, right, contract, preferred_element_type=jnp.float32)
            terms += [both[0:24, 0:128], both[24:48, 128:256]]
        past = table[row, jnp.maximum(base - 1, 0)]
        for u in range(UNROLL):
            same = (words[u] >> 13) == (past >> 13)
            past = words[u]
            acc = terms[u] + jnp.where(same, acc, 0.0)
            runs[base + u] = acc
        return acc

    return lax.fori_loop(first, last, body, acc)


def kernel(
    x_hbm, pattern_hbm, count, tiles_hbm, out_ref,
    raw, pattern, padded, table_v, table, tiles, own, held, runs,
    col, col_scale, row, leaving, col_got, scale_got, pieces,
    load, tile_sem, x_send, x_recv, col_send, col_recv, scale_send, scale_recv, row_send, row_recv,
):
    i, k = lax.axis_index("diag"), lax.axis_index("tri")
    x, z_hi = k & 3, k >> 2
    source = (i - k) & 31
    home = k == 0
    from_half = half_of(i, z_hi, x)
    giver = {"diag": source, "tri": from_half * 4 + x}
    takers = []
    for h in (0, 1):
        user = (i + 4 * h + x) & 31
        takes = (half_of(user, h, x) == z_hi) & jnp.logical_not((h * 4 + x) == 0)
        takers.append((takes, {"diag": user, "tri": h * 4 + x}))
    turn = 1 - 2 * (i & 1)
    peers = [((1 - z_hi) * 4 + ((x + turn * d) & 3)) for d in (2, 1, 3, 0)] + [z_hi * 4 + ((x + turn * d) & 3) for d in (2, 1, 3)]

    get_pattern = pltpu.make_async_copy(pattern_hbm, pattern, load.at[0])
    get_x = pltpu.make_async_copy(x_hbm, raw, load.at[1])
    get_pattern.start()
    get_x.start()
    each = 192 // CHUNKS
    get_tiles = []
    for n in range(CHUNKS):
        part = pl.ds(n * each, each)
        get_tiles.append(pltpu.make_async_copy(tiles_hbm.at[part], tiles.at[part], tile_sem.at[n]))
        get_tiles[n].start()

    barrier = pltpu.get_barrier_semaphore()
    expected = jnp.int32(7)
    for takes, user in [*takers, (jnp.logical_not(home), giver)]:
        expected = expected + takes.astype(jnp.int32)

        @pl.when(takes)
        def _():
            pl.semaphore_signal(barrier, inc=1, device_id=user, device_id_type=MESH)
    for peer in peers:
        pl.semaphore_signal(barrier, inc=1, device_id={"diag": i, "tri": peer}, device_id_type=MESH)

    get_x.wait()
    whole = jnp.concatenate([raw[p] for p in range(12)], 0)
    for c in range(32):
        own[c] = whole[:, c * 128 : (c + 1) * 128]
    meeting = ((MEETINGS >> (3 * (((i >> 1) & 3) + 4 * z_hi))) & 7) - 1
    give = []
    for h in (0, 1):
        takes, user = takers[h]
        give.append(
            pltpu.make_async_remote_copy(own, held, x_send.at[h], x_recv, device_id=user, device_id_type=MESH)
        )
    keep = pltpu.make_async_copy(own, held, x_recv)

    def meet(step):
        @pl.when(step == meeting)
        def _():
            pl.semaphore_wait(barrier, expected)
            for h in (0, 1):
                pl.when(takers[h][0])(give[h].start)
            pl.when(home)(keep.start)

    meet(-1)
    get_pattern.wait()
    padded[:, 0:192] = pattern[...]
    padded[:, 192:256] = jnp.zeros((2, 64), jnp.int32)
    pairs = padded[...]
    live = count[0, 0]
    col_order, col_ends = tables(pairs, live, False)
    row_order, row_ends = tables(pairs, live, True)
    table_v[...] = jnp.concatenate([col_order, col_ends, row_order, row_ends] * 2, 0)
    runs[192] = jnp.zeros((24, 128), jnp.float32)
    col_got[2] = jnp.zeros((32, 24, 128), jnp.int16)
    scale_got[2] = jnp.zeros((24, 128), jnp.float32)

    get_table = pltpu.make_async_copy(table_v, table, load.at[2])
    get_table.start()
    get_table.wait()

    for copy in get_tiles:
        copy.wait()
    acc = jnp.zeros((24, 128), jnp.float32)
    visit(False, 0, 0, 192 // COL_UNROLL, acc, table, tiles, own, runs, meet)
    lane = lax.broadcasted_iota(jnp.int32, (24, 128), 1)
    scales = jnp.zeros((24, 128), jnp.float32)
    for t in range(8):
        codes, scale = coded([runs[table[1, t * 4 + j]] for j in range(4)])
        for j in range(4):
            col[t * 4 + j] = codes[j]
        scales = jnp.where(lane == t, scale, scales)
    col_scale[...] = scales

    back = [
        pltpu.make_async_remote_copy(
            col, col_got.at[z_hi], col_send, col_recv.at[z_hi], device_id=giver, device_id_type=MESH
        ),
        pltpu.make_async_remote_copy(
            col_scale, scale_got.at[z_hi], scale_send, scale_recv.at[z_hi], device_id=giver, device_id_type=MESH
        ),
    ]

    @pl.when(jnp.logical_not(home))
    def _():
        for copy in back:
            copy.start()
        pltpu.make_async_remote_copy(own, held, x_send.at[0], x_recv, device_id=giver, device_id_type=MESH).wait_recv()

    keep_col = pltpu.make_async_copy(col, col_got.at[0], col_recv.at[0])
    keep_scale = pltpu.make_async_copy(col_scale, scale_got.at[0], scale_recv.at[0])

    @pl.when(home)
    def _():
        keep_col.start()
        keep_scale.start()
        keep.wait()

    visit(True, 2, 0, 192 // ROW_UNROLL, acc, table, tiles, held, runs)
    @pl.when(home)
    def _():
        keep_col.wait()
        keep_scale.wait()

    slots = []
    for h in (0, 1):
        takes, user = takers[h]
        filled = takes if h else takes | home
        slots.append(jnp.where(filled, h, 2))

        @pl.when(takes)
        def _():
            pltpu.make_async_remote_copy(
                col, col_got.at[h], col_send, col_recv.at[h], device_id=user, device_id_type=MESH
            ).wait_recv()
            pltpu.make_async_remote_copy(
                col_scale, scale_got.at[h], scale_send, scale_recv.at[h], device_id=user, device_id_type=MESH
            ).wait_recv()

    scatter = []
    scales = [scale_got[slot] for slot in slots]
    for n, peer in enumerate([*peers, k]):
        part = [jnp.sum(jnp.where(lane == peer, s, 0.0), axis=1, keepdims=True) for s in scales]
        part = [jnp.broadcast_to(s, (24, 128)) for s in part]
        totals = []
        for j in range(4):
            p = peer * 4 + j
            total = runs[table[3, p]]
            for slot, scale in zip(slots, part):
                total = total + col_got[slot, p].astype(jnp.int32).astype(jnp.float32) * scale
            totals.append(total)
        if n == 7:
            for j in range(4):
                row[j] = totals[j]
            break
        for j, codes in enumerate(packed(totals)):
            leaving[n, j] = codes
        copy = pltpu.make_async_remote_copy(
            leaving.at[n],
            pieces.at[n],
            row_send.at[n],
            row_recv.at[n],
            device_id={"diag": i, "tri": peer},
            device_id_type=MESH,
        )
        copy.start()
        scatter.append(copy)

    totals = [row[j] for j in range(4)]
    for n in (4, 5, 6, 3, 0, 1, 2):
        scatter[n].wait_recv()
        totals = [a + b for a, b in zip(totals, unpacked(pieces.at[n]))]
    for j, total in enumerate(totals):
        for p in range(12):
            out_ref[p, :, j * 128 : (j + 1) * 128] = total[2 * p : 2 * p + 2, :]
    for h in (0, 1):
        takes, user = takers[h]

        @pl.when(takes)
        def _():
            give[h].wait_send()

    @pl.when(jnp.logical_not(home))
    def _():
        for copy in back:
            copy.wait_send()
    for copy in scatter:
        copy.wait_send()


def local(trial_sets, tile_values, tile_pattern, tile_count):
    sets, vecs, rows = trial_sets.shape
    tri = lax.axis_size("tri")
    columns = sets * vecs
    slots, size = tile_values.shape[2:4]
    blocks = rows // size
    f32, bf16, i32 = jnp.float32, jnp.bfloat16, jnp.int32
    dma = pltpu.SemaphoreType.DMA
    block = (columns, size)
    hbm = functools.partial(pltpu.with_memory_space_constraint, memory_space=pltpu.HBM)
    out = pl.pallas_call(
        kernel,
        out_shape=jax.ShapeDtypeStruct((vecs, sets, rows // tri), f32),
        in_specs=[
            pl.BlockSpec(memory_space=pltpu.HBM),
            pl.BlockSpec(memory_space=pltpu.HBM),
            pl.BlockSpec(memory_space=pltpu.SMEM),
            pl.BlockSpec(memory_space=pltpu.HBM),
        ],
        out_specs=pl.BlockSpec(memory_space=pltpu.VMEM),
        scratch_shapes=[
            pltpu.VMEM((vecs, sets, rows), bf16),
            pltpu.VMEM((2, slots), i32),
            pltpu.VMEM((2, 256), i32),
            pltpu.VMEM((8, 256), i32),
            pltpu.SMEM((8, 256), i32),
            pltpu.VMEM((slots, size, size), bf16),
            pltpu.VMEM((blocks, *block), bf16),
            pltpu.VMEM((blocks, *block), bf16),
            pltpu.VMEM((slots + 8, *block), f32),
            pltpu.VMEM((blocks, *block), jnp.int16),
            pltpu.VMEM(block, f32),
            pltpu.VMEM((4, *block), f32),
            pltpu.VMEM((7, 5, *block), jnp.int16),
            pltpu.VMEM((3, blocks, *block), jnp.int16),
            pltpu.VMEM((3, *block), f32),
            pltpu.VMEM((7, 5, *block), jnp.int16),
            dma((3,)),
            dma((CHUNKS,)),
            dma((2,)),
            dma(()),
            dma(()),
            dma((2,)),
            dma(()),
            dma((2,)),
            dma((7,)),
            dma((7,)),
        ],
        compiler_params=pltpu.CompilerParams(
            collective_id=0, has_side_effects=True, vmem_limit_bytes=40 << 20
        ),
        name="block_products",
    )(hbm(trial_sets.transpose(1, 0, 2)), hbm(tile_pattern[0, 0]), tile_count, hbm(tile_values[0, 0]))
    return out.transpose(1, 0, 2)


def solution(mesh):
    return jax.shard_map(
        local,
        mesh=mesh,
        in_specs=(
            P(None, None, "diag"),
            P("diag", "tri", None, None, None),
            P("diag", "tri", None, None),
            P("diag", "tri"),
        ),
        out_specs=P(None, None, ("diag", "tri")),
        check_vma=False,
    )
```
